256 devices in a mesh: span: 8 (over z_lo, y), ulysses: 32 (over x, z_hi, core).
Axes of the slice: x: 4, y: 4, z: 8 (z_hi: 4, z_lo: 2; z = z_hi * 2 + z_lo), core: 2. Of those that a mesh axis runs over, the one named last changes fastest.
Arguments:
- query: bfloat16 [32768, 4096], P(('span', 'ulysses')), may hold values from -32 to 32
- key: bfloat16 [32768, 1024], P(('span', 'ulysses')), may hold values from -6 to 6
- value: bfloat16 [32768, 1024], P(('span', 'ulysses')), may hold values from -6 to 6
- d_out: bfloat16 [32768, 4096], P(('span', 'ulysses')), may hold values from -6 to 6
Outputs:
- attended: bfloat16 [32768, 4096], P(('span', 'ulysses'))
- grad_query: float32 [1024, 4096], P(('span', 'ulysses'))
- grad_key: float32 [1024, 1024], P(('span', 'ulysses'))
- grad_value: float32 [1024, 1024], P(('span', 'ulysses'))
The draws below stay inside these ranges and needn't reach their ends.
All inputs are finite; a program needn't handle non-finite values.
Results may differ from the reference program's by a relative error of at most 0.0048.
Values may be sent and summed in bfloat16 or wider, within the bound.
A program may use at most 256 MiB of HBM per device.

```python
import math
import jax
import jax.numpy as jnp
import numpy as np
from jax import lax

H = 32
HD = 128
KVH = 8
INTERVAL = 32
SPAN_LEN = 4096
BEACONS = 128
TOKENS = 32768
ALL_BEACONS = 1024
N_SPAN = 8


def pair_fields(key):
    base = jax.random.fold_in(key, 4242)
    key_q, key_k = jax.random.split(base, 2)
    kfield = jnp.clip(jax.random.normal(key_k, (TOKENS, KVH, HD)), -6.0, 6.0)
    qfield = jnp.clip(jax.random.normal(key_q, (TOKENS, H, HD)), -6.0, 6.0)
    return (qfield.reshape(TOKENS, H * HD), kfield.reshape(TOKENS, KVH * HD))


def draw_query(key, part):
    return pair_fields(key)[0].astype(jnp.bfloat16)


def draw_key(key, part):
    return pair_fields(key)[1].astype(jnp.bfloat16)


def block_scale(stream_key, extent, pieces, smallest, top_value):
    def one(axis_at, shards_of):
        heights = jax.random.uniform(jax.random.fold_in(jax.random.fold_in(stream_key, 6), axis_at), (shards_of,), jnp.float32, smallest / len(pieces), top_value / len(pieces))
        return jnp.repeat(jnp.exp(heights), extent[axis_at] // shards_of).reshape((-1,) + (1,) * (len(extent) - axis_at - 1))

    loudness = one(*pieces[0])
    for cut in pieces[1:]:
        loudness = loudness * one(*cut)
    return loudness


def noise(own_key, extent, deviation, bound, shards=(), held_as=jnp.bfloat16):
    level = block_scale(own_key, extent, shards, -0.22, 0.18) if shards else 1.0
    values = jax.random.normal(own_key, extent, jnp.float32) * deviation * level
    return jnp.minimum(jnp.maximum(values, -bound), bound).astype(held_as)


def setup_inputs(seed: int = 0) -> dict:
    seeds = jax.random.split(jax.random.key(seed), 5)
    return {
        "query": draw_query(jax.random.fold_in(seeds[4], 71), 0),
        "key": draw_key(jax.random.fold_in(seeds[4], 71), 0),
        "value": noise(seeds[2], (TOKENS, KVH * HD), 1.0, 6.0, ((0, 256),)),
        "d_out": noise(seeds[3], (TOKENS, H * HD), 1.0, 6.0, ((0, 256),)),
    }


def one_head(q, keys, vals, grad, prior):
    length = q.shape[0]
    scale = 1.0 / math.sqrt(HD)
    scores = jnp.dot(q, keys.T, preferred_element_type=jnp.float32) * scale
    column = jnp.arange(keys.shape[0])[None, :]
    place = jnp.arange(length)[:, None]
    valid = (column < prior) | (column - prior <= place)
    scores = jnp.where(valid, scores, -jnp.inf)
    peak = lax.optimization_barrier(jnp.max(scores, axis=1, keepdims=True))
    expo = jnp.exp(scores - peak)
    probs = expo / lax.optimization_barrier(jnp.sum(expo, axis=1, keepdims=True))
    probs_b = probs.astype(jnp.bfloat16)
    out_b = jnp.dot(probs_b, vals, preferred_element_type=jnp.float32).astype(jnp.bfloat16)
    delta = lax.optimization_barrier(jnp.sum(grad.astype(jnp.float32) * out_b.astype(jnp.float32), axis=1, keepdims=True))
    dprobs = jnp.dot(grad, vals.T, preferred_element_type=jnp.float32)
    dscore = (probs * (dprobs - delta)).astype(jnp.bfloat16)
    picks = np.concatenate([np.arange(prior), prior + np.arange(BEACONS) * INTERVAL + INTERVAL - 1]).astype(np.int32)
    grad_keys = jnp.dot(dscore[:, picks].T, q, preferred_element_type=jnp.float32) * scale
    grad_vals = jnp.dot(probs_b[:, picks].T, grad, preferred_element_type=jnp.float32)
    grad_rows = jnp.dot(dscore[INTERVAL - 1::INTERVAL], keys, preferred_element_type=jnp.float32) * scale
    return (out_b, grad_rows, grad_keys, grad_vals)

def reference(query, key, value, d_out):
    repeat = H // KVH
    q_all = query.reshape(N_SPAN, SPAN_LEN, H, HD)
    k_all = key.reshape(N_SPAN, SPAN_LEN, KVH, HD)
    v_all = value.reshape(N_SPAN, SPAN_LEN, KVH, HD)
    g_all = d_out.reshape(N_SPAN, SPAN_LEN, H, HD)
    beacon_k = k_all[:, INTERVAL - 1::INTERVAL]
    beacon_v = v_all[:, INTERVAL - 1::INTERVAL]
    total_k = jnp.zeros((ALL_BEACONS, H, HD), jnp.float32)
    total_v = jnp.zeros((ALL_BEACONS, H, HD), jnp.float32)
    outputs = []
    query_grads = []
    for span_id in range(N_SPAN):
        prior = span_id * BEACONS
        keys_c = jnp.concatenate([beacon_k[:span_id].reshape(prior, KVH, HD), k_all[span_id]], 0)
        vals_c = jnp.concatenate([beacon_v[:span_id].reshape(prior, KVH, HD), v_all[span_id]], 0)
        keys_h = jnp.repeat(keys_c.transpose(1, 0, 2), repeat, axis=0)
        vals_h = jnp.repeat(vals_c.transpose(1, 0, 2), repeat, axis=0)
        q_h = q_all[span_id].transpose(1, 0, 2)
        g_h = g_all[span_id].transpose(1, 0, 2)
        result = lax.map(lambda items, prior=prior: one_head(items[0], items[1], items[2], items[3], prior), (q_h, keys_h, vals_h, g_h))
        out_b, rows, grad_keys, grad_vals = result
        outputs.append(out_b.transpose(1, 0, 2).reshape(SPAN_LEN, H * HD))
        query_grads.append(rows.transpose(1, 0, 2).reshape(BEACONS, H * HD))
        total_k = total_k.at[:prior + BEACONS].add(grad_keys.transpose(1, 0, 2))
        total_v = total_v.at[:prior + BEACONS].add(grad_vals.transpose(1, 0, 2))
    grad_key = total_k.reshape(ALL_BEACONS, KVH, repeat, HD).sum(axis=2).reshape(ALL_BEACONS, KVH * HD)
    grad_value = total_v.reshape(ALL_BEACONS, KVH, repeat, HD).sum(axis=2).reshape(ALL_BEACONS, KVH * HD)
    return (jnp.concatenate(outputs, 0), jnp.concatenate(query_grads, 0), grad_key, grad_value)
```

```python
import functools
import math

import jax
import jax.numpy as jnp
from jax import lax
from jax.experimental import pallas as pl
from jax.experimental.pallas import tpu as pltpu
from jax.sharding import PartitionSpec as P

NX, NZ, NC, NS = 4, 4, 2, 8
NG = NX * NC
HD = 128
REP = 4
TOK = 128
BLK = NC * TOK
STEP = NZ * BLK
LOC = NX * STEP
ROWS = REP * BLK
BEA = 32
BSP = BEA * NZ
ALLB = NS * BSP
PLANE = NS * NZ
SCALE = 1.0 / math.sqrt(HD)
LOG2E = 1.4426950408889634
C2 = SCALE * LOG2E
MESH = pl.DeviceIdType.MESH
COMM = True
FWD = True
BWD = True


def dot_t(a, b):
    return lax.dot_general(a, b, (((1,), (1,)), ((), ())), preferred_element_type=jnp.float32)


def dot_n(a, b):
    return lax.dot_general(a, b, (((1,), (0,)), ((), ())), preferred_element_type=jnp.float32)


def iota(shape, dim):
    return lax.broadcasted_iota(jnp.int32, shape, dim)


def fused(
    q_hbm, k_hbm, v_hbm, do_hbm,
    out_hbm, gq_ref, gk_ref, gv_ref,
    kv, kvb, bst, qg, dog, outg, q4, do4, sbuf, mx, acc, lse_row, del_row,
    dk_acc, dv_acc, gacc, slots, tiles, gkv_in, dq_st, gq_in,
    kx_s, kx_r, vx_s, vx_r, q_s, q_r, do_s, do_r, z_s, z_r, zr_s, b_s, b_r,
    o_s, o_r, g_s, g_r, t_s, t_r, d_s, d_r,
):
    c = lax.axis_index("span")
    u = lax.axis_index("ulysses")
    x = u // (NZ * NC)
    z = (u // NC) % NZ
    core = u % NC
    g = x * NC + core
    me = c * NZ + z
    zp, zm = (z + 1) % NZ, (z + NZ - 1) % NZ

    def uly(grp, zz):
        return (grp // NC) * (NZ * NC) + zz * NC + grp % NC

    def in_group(grp):
        return {"span": c, "ulysses": uly(grp, z)}

    def in_plane(s):
        return {"span": s // NZ, "ulysses": uly(g, s % NZ)}

    def remote(src, dst, ssem, rsem, dev):
        return pltpu.make_async_remote_copy(
            src_ref=src, dst_ref=dst, send_sem=ssem, recv_sem=rsem, device_id=dev, device_id_type=MESH
        )

    def arrived(dst, sem):
        pltpu.make_async_copy(dst, dst, sem).wait()

    def kv_rows(grp, zz):
        return pl.ds((grp // NC) * STEP + zz * BLK + (grp % NC) * TOK, TOK)

    def piece_k(grp):
        return kv.at[kv_rows(grp, z), pl.ds(0, HD)]

    def piece_v(grp):
        return kv.at[kv_rows(grp, z), pl.ds(HD, HD)]

    def piece_q(buf, grp):
        return buf.at[pl.ds(grp * TOK, TOK), :]

    def x_copies(to, src_k=True):
        cols = pl.ds(pl.multiple_of(to * HD, HD), HD)
        wide = pl.ds(pl.multiple_of(to * REP * HD, REP * HD), REP * HD)
        return (
            (k_hbm.at[:, cols], piece_k(g), kx_s.at[to], kx_r.at[g]),
            (v_hbm.at[:, cols], piece_v(g), vx_s.at[to], vx_r.at[g]),
            (q_hbm.at[:, wide], piece_q(qg, g), q_s.at[to], q_r.at[g]),
            (do_hbm.at[:, wide], piece_q(dog, g), do_s.at[to], do_r.at[g]),
        )

    def z_rows(xx, zz):
        return pl.ds(xx * STEP + zz * BLK, BLK)

    def z_piece(xx, zz, lo, width):
        return kv.at[z_rows(xx, zz), pl.ds(lo, width)]

    def z_dev(zz):
        return {"span": c, "ulysses": uly(g, zz)}

    def z_send(xx, way):
        to = zp if way == 0 else zm
        part = z_piece(xx, z, 0, 2 * HD)
        return remote(part, part, z_s.at[xx, way], z_r.at[xx, way], z_dev(to))

    def z_relay(xx, way):
        to, of = (zp, zm) if way == 0 else (zm, zp)
        part = z_piece(xx, of, way * HD, HD)
        return remote(part, part, zr_s.at[xx, way], z_r.at[xx, 2 + way], z_dev(to))

    def b_rows(s):
        return kvb.at[pl.ds(pl.multiple_of(s * BEA, BEA), BEA), pl.ds(0, 2 * HD)]

    def b_send(s):
        return remote(bst, b_rows(me), b_s.at[s], b_r.at[me], in_plane(s))

    def o_send(grp):
        dst = out_hbm.at[:, pl.ds(pl.multiple_of(g * REP * HD, REP * HD), REP * HD)]
        return remote(piece_q(outg, grp), dst, o_s.at[grp], o_r.at[g], in_group(grp))

    def g_send(s):
        return remote(gacc.at[s], slots.at[me], g_s.at[s], g_r.at[me], in_plane(s))

    def t_send(grp):
        return remote(tiles.at[grp], gkv_in.at[g], t_s.at[grp], t_r.at[g], in_group(grp))

    def d_send(grp):
        return remote(
            dq_st.at[pl.ds(pl.multiple_of(grp * 16, 16), 16), :],
            gq_in.at[pl.ds(pl.multiple_of(g * 16, 16), 16), :],
            d_s.at[grp], d_r.at[g], in_group(grp),
        )

    def others(body):
        for k in range(1, NG):
            body((g + k) % NG)

    def plane(lo, hi, body):
        def one(s, carry):
            @pl.when(s != me)
            def _():
                body(s)

            return carry

        lax.fori_loop(lo, hi, one, 0)

    if COMM:
        barrier = pltpu.get_barrier_semaphore()
        others(lambda grp: pl.semaphore_signal(barrier, inc=1, device_id=in_group(grp), device_id_type=MESH))
        plane(0, PLANE, lambda s: pl.semaphore_signal(barrier, inc=1, device_id=in_plane(s), device_id_type=MESH))
        pl.semaphore_wait(barrier, NG - 1 + PLANE - 1)

    mine = x_copies(g)
    for which in range(4):
        src, dst, _, rsem = mine[which]
        pltpu.make_async_copy(src, dst, rsem).start()
        if COMM:
            others(lambda grp, which=which: remote(*x_copies(grp)[which], in_group(grp)).start())

    kv[:, pl.ds(2 * HD, HD)] = jnp.ones((LOC, HD), jnp.bfloat16)
    kvb[:, pl.ds(2 * HD, HD)] = jnp.ones((ALLB, HD), jnp.bfloat16)

    def wait_group(buf_piece, sem, grp):
        arrived(buf_piece(grp), sem.at[grp])

    for xx in range(NX):
        for cc in range(NC):
            grp = xx * NC + cc
            if COMM:
                wait_group(piece_k, kx_r, grp)
                wait_group(piece_v, vx_r, grp)
        if COMM:
            z_send(xx, 0).start()
            z_send(xx, 1).start()
    if not COMM:
        wait_group(piece_k, kx_r, g)
        wait_group(piece_v, vx_r, g)

    picked = jnp.zeros((BEA, 2 * HD), jnp.float32)
    for xx in range(NX):
        row, col = iota((BEA, BLK), 0), iota((BEA, BLK), 1)
        hot = (row * 32 + 31 == col + xx * BLK).astype(jnp.bfloat16)
        picked = picked + dot_n(hot, kv[z_rows(xx, z), pl.ds(0, 2 * HD)])
    bst[...] = picked.astype(jnp.bfloat16)
    kvb[pl.ds(pl.multiple_of(me * BEA, BEA), BEA), pl.ds(0, 2 * HD)] = bst[...]
    if COMM:
        plane(c * NZ, PLANE, lambda s: b_send(s).start())
        for xx in range(NX):
            arrived(z_piece(xx, zm, 0, 2 * HD), z_r.at[xx, 0])
            z_relay(xx, 0).start()
            arrived(z_piece(xx, zp, 0, 2 * HD), z_r.at[xx, 1])
            z_relay(xx, 1).start()
        plane(0, (c + 1) * NZ, lambda s: arrived(b_rows(s), b_r.at[s]))

    n_prior = (c + 1) // 2
    z2 = (z + 2) % NZ

    def block(i, carry):
        for cc in range(NC):
            grp = i * NC + cc
            if COMM:
                wait_group(functools.partial(piece_q, qg), q_r, grp)
            else:
                pl.when(grp == g)(lambda: wait_group(functools.partial(piece_q, qg), q_r, g))
        if COMM:
            arrived(z_piece(i, z2, 0, HD), z_r.at[i, 2])
            arrived(z_piece(i, z2, HD, HD), z_r.at[i, 3])
        for h in range(REP):
            q4[i, pl.ds(h * BLK, BLK), :] = qg[pl.ds(i * BLK, BLK), pl.ds(h * HD, HD)]
        if not FWD:
            return carry
        mx[...] = jnp.full((ROWS, HD), -jnp.inf, jnp.float32)

        def widest(s, rows):
            top = s[:, :HD]
            for t in range(1, s.shape[1] // HD):
                top = jnp.maximum(top, s[:, t * HD : (t + 1) * HD])
            mx[rows, :] = jnp.maximum(mx[rows, :], top)

        def score_prior(jp, cr):
            keys = kvb[pl.ds(pl.multiple_of(jp * 256, 256), 256), pl.ds(0, HD)]
            for h in range(REP):
                rows = pl.ds(h * BLK, BLK)
                s = dot_t(q4[i, rows, :], keys)
                s = jnp.where(iota(s.shape, 1) < c * BSP - jp * 256, s, -jnp.inf)
                sbuf[0, rows, pl.ds(pl.multiple_of(jp * 256, 256), 256)] = s
                widest(s, rows)
            return cr

        lax.fori_loop(0, n_prior, score_prior, 0)

        def score(j, masked):
            keys = kv[pl.ds(pl.multiple_of(j * STEP, STEP), STEP), pl.ds(0, HD)]
            for h in range(REP):
                rows = pl.ds(h * BLK, BLK)
                s = dot_t(q4[i, rows, :], keys)
                if masked:
                    s = jnp.where(iota(s.shape, 1) - iota(s.shape, 0) <= z * BLK, s, -jnp.inf)
                sbuf[1 + j, rows, :] = s
                widest(s, rows)

        def score_full(j, cr):
            score(j, False)
            return cr

        lax.fori_loop(0, i, score_full, 0)
        score(i, True)

        peak = jnp.max(mx[...], axis=1, keepdims=True) * C2
        mx[...] = jnp.broadcast_to(peak, (ROWS, HD))
        acc[...] = jnp.zeros((ROWS, 2 * HD), jnp.float32)

        def spread(s, rows):
            m = mx[rows, :]
            return jnp.concatenate(
                [jnp.exp2(s[:, t * HD : (t + 1) * HD] * C2 - m) for t in range(s.shape[1] // HD)], axis=1
            ).astype(jnp.bfloat16)

        def mix_prior(jp, cr):
            at = pl.ds(pl.multiple_of(jp * 256, 256), 256)
            vals = kvb[at, pl.ds(HD, 2 * HD)]
            for h in range(REP):
                rows = pl.ds(h * BLK, BLK)
                acc[rows, :] += dot_n(spread(sbuf[0, rows, at], rows), vals)
            return cr

        lax.fori_loop(0, n_prior, mix_prior, 0)

        def mix(j, cr):
            vals = kv[pl.ds(pl.multiple_of(j * STEP, STEP), STEP), pl.ds(HD, 2 * HD)]
            for h in range(REP):
                rows = pl.ds(h * BLK, BLK)
                acc[rows, :] += dot_n(spread(sbuf[1 + j, rows, :], rows), vals)
            return cr

        lax.fori_loop(0, i + 1, mix, 0)
        eye = iota((HD, HD), 0) == iota((HD, HD), 1)
        for h in range(REP):
            rows = pl.ds(h * BLK, BLK)
            total = acc[rows, pl.ds(HD, HD)]
            outg[pl.ds(i * BLK, BLK), pl.ds(h * HD, HD)] = (acc[rows, pl.ds(0, HD)] / total).astype(jnp.bfloat16)
            lse = mx[rows, :] + jnp.log2(total)
            for t in range(BLK // HD):
                part = jnp.where(eye, lse[t * HD : (t + 1) * HD], 0.0)
                lse_row[i, :, pl.ds(h * BLK + t * HD, HD)] = jnp.sum(part, axis=0, keepdims=True)
        for cc in range(NC):
            grp = i * NC + cc

            @pl.when(grp != g)
            def _():
                if COMM:
                    o_send(grp).start()

            @pl.when(grp == g)
            def _():
                cols = pl.ds(pl.multiple_of(g * REP * HD, REP * HD), REP * HD)
                pltpu.make_async_copy(piece_q(outg, g), out_hbm.at[:, cols], o_r.at[g]).start()

        return carry

    lax.fori_loop(0, NX, block, 0)

    def deltas(i, carry):
        for cc in range(NC):
            grp = i * NC + cc
            if COMM:
                wait_group(functools.partial(piece_q, dog), do_r, grp)
            else:
                pl.when(grp == g)(lambda: wait_group(functools.partial(piece_q, dog), do_r, g))
        eye = iota((HD, HD), 0) == iota((HD, HD), 1)
        for h in range(REP):
            cols = pl.ds(h * HD, HD)
            grad = dog[pl.ds(i * BLK, BLK), cols]
            do4[i, pl.ds(h * BLK, BLK), :] = grad
            prod = grad.astype(jnp.float32) * outg[pl.ds(i * BLK, BLK), cols].astype(jnp.float32)
            total = jnp.broadcast_to(jnp.sum(prod, axis=1, keepdims=True), prod.shape)
            for t in range(BLK // HD):
                part = jnp.where(eye, total[t * HD : (t + 1) * HD], 0.0)
                del_row[i, :, pl.ds(h * BLK + t * HD, HD)] = jnp.sum(part, axis=0, keepdims=True)
        return carry

    lax.fori_loop(0, NX, deltas, 0)

    own = iota((256, 1), 0)

    def back(cp, carry):
        at = pl.ds(pl.multiple_of(cp * 256, 256), 256)
        rel = own + cp * 256 - c * BSP
        place = (rel % 32 // 8) * STEP + (rel // 32) * BLK + (rel % 8) * 32 + 31
        place = jnp.where(rel < 0, -1, jnp.where(rel >= BSP, LOC, place))
        dk_acc[...] = jnp.zeros((256, HD), jnp.float32)
        dv_acc[...] = jnp.zeros((256, HD), jnp.float32)

        def one(i, cr):
            keys, vals = kvb[at, pl.ds(0, HD)], kvb[at, pl.ds(HD, HD)]
            qs, gs = q4[i], do4[i]
            s = dot_t(keys, qs)
            here = iota((1, ROWS), 1) % BLK + i * STEP + z * BLK
            p = jnp.where(place <= here, jnp.exp2(s * C2 - lse_row[i]), 0.0)
            dp = dot_t(vals, gs)
            ds = (p * (dp - del_row[i])).astype(jnp.bfloat16)
            dv_acc[...] += dot_n(p.astype(jnp.bfloat16), gs)
            dk_acc[...] += dot_n(ds, qs)
            return cr

        lax.fori_loop(0, NX, one, 0)
        for a in range(2):
            for zz in range(NZ):
                s = (cp * 2 + a) * NZ + zz
                rows = pl.ds(a * BSP + zz * BEA, BEA)
                gacc[s, pl.ds(0, BEA), :] = dk_acc[rows, :] * SCALE
                gacc[s, pl.ds(BEA, BEA), :] = dv_acc[rows, :]
        if COMM:
            plane(cp * 2 * NZ, jnp.minimum(cp * 2 + 2, c + 1) * NZ, lambda s: g_send(s).start())
        return carry

    if BWD:
        lax.fori_loop(0, (c + 2) // 2, back, 0)

        row = iota((HD, 1), 0)
        dest, head, num = row // 16, (row // 4) % 4, row % 4
        spot = head * BLK + (dest % NC) * TOK + num * 32 + 31
        here = (dest // NC) * STEP + z * BLK + (dest % NC) * TOK + num * 32 + 31
        qb = jnp.zeros((HD, HD), jnp.float32)
        gb = jnp.zeros((HD, HD), jnp.float32)
        lse_b = jnp.zeros((HD, 1), jnp.float32)
        del_b = jnp.zeros((HD, 1), jnp.float32)
        for i in range(NX):
            pick = (iota((HD, ROWS), 1) == spot) & (dest // NC == i)
            hot = pick.astype(jnp.bfloat16)
            qb = qb + dot_n(hot, q4[i])
            gb = gb + dot_n(hot, do4[i])
            lse_b = lse_b + jnp.sum(jnp.where(pick, lse_row[i], 0.0), axis=1, keepdims=True)
            del_b = del_b + jnp.sum(jnp.where(pick, del_row[i], 0.0), axis=1, keepdims=True)
        qb = qb.astype(jnp.bfloat16)
        gb = gb.astype(jnp.bfloat16)

        def dq_part(keys, vals, seen):
            s = dot_t(qb, keys)
            p = jnp.where(seen(iota(s.shape, 1)), jnp.exp2(s * C2 - lse_b), 0.0)
            ds = (p * (dot_t(gb, vals) - del_b)).astype(jnp.bfloat16)
            return dot_n(ds, keys)

        def dq_prior(jp, total):
            at = pl.ds(pl.multiple_of(jp * 256, 256), 256)
            seen = lambda col: col < c * BSP - jp * 256
            return total + dq_part(kvb[at, pl.ds(0, HD)], kvb[at, pl.ds(HD, HD)], seen)

        dq = lax.fori_loop(0, n_prior, dq_prior, jnp.zeros((HD, HD), jnp.float32))

        def dq_local(j, total):
            at = pl.ds(pl.multiple_of(j * STEP, STEP), STEP)
            seen = lambda col: col + j * STEP <= here
            return total + dq_part(kv[at, pl.ds(0, HD)], kv[at, pl.ds(HD, HD)], seen)

        dq = lax.fori_loop(0, NX, dq_local, dq)
        dq_st[...] = dq * SCALE
    mine_rows = pl.ds(pl.multiple_of(g * 16, 16), 16)
    gq_in[mine_rows, :] = dq_st[mine_rows, :]
    if COMM:
        others(lambda grp: d_send(grp).start())

    dk_acc[pl.ds(0, 2 * BEA), :] = gacc[me]
    if COMM:

        def add(s):
            arrived(slots.at[s], g_r.at[s])
            dk_acc[pl.ds(0, 2 * BEA), :] += slots[s]

        plane(c * NZ, PLANE, add)
    for d in range(NG):
        tiles[d, pl.ds(0, 4), :] = dk_acc[pl.ds(d * 4, 4), :]
        tiles[d, pl.ds(4, 4), :] = dk_acc[pl.ds(BEA + d * 4, 4), :]
    gkv_in[g] = tiles[g]
    if COMM:
        others(lambda grp: t_send(grp).start())
        others(lambda grp: arrived(gq_in.at[pl.ds(pl.multiple_of(grp * 16, 16), 16), :], d_r.at[grp]))
        others(lambda grp: arrived(gkv_in.at[grp], t_r.at[grp]))
    for grp in range(NG):
        gk_ref[:, pl.ds(grp * HD, HD)] = gkv_in[grp, pl.ds(0, 4), :]
        gv_ref[:, pl.ds(grp * HD, HD)] = gkv_in[grp, pl.ds(4, 4), :]
        for h in range(REP):
            gq_ref[:, pl.ds((grp * REP + h) * HD, HD)] = gq_in[pl.ds(grp * 16 + h * 4, 4), :]

    def out_cols(grp):
        return out_hbm.at[:, pl.ds(pl.multiple_of(grp * REP * HD, REP * HD), REP * HD)]

    if FWD:
        arrived(out_cols(g), o_r.at[g])
    if COMM:
        others(lambda grp: arrived(out_cols(grp), o_r.at[grp]))
        for which in range(4):
            others(lambda grp, which=which: remote(*x_copies(grp)[which], in_group(grp)).wait_send())
        for xx in range(NX):
            for way in range(2):
                z_send(xx, way).wait_send()
                z_relay(xx, way).wait_send()
        plane(c * NZ, PLANE, lambda s: b_send(s).wait_send())
        others(lambda grp: o_send(grp).wait_send())
        plane(0, (c + 1) * NZ, lambda s: g_send(s).wait_send())
        others(lambda grp: d_send(grp).wait_send())
        others(lambda grp: t_send(grp).wait_send())


def on_device(query, key, value, d_out):
    f32, b16 = jnp.float32, jnp.bfloat16
    vm = pltpu.VMEM
    dma = pltpu.SemaphoreType.DMA
    scratch = [
        vm((LOC, 3 * HD), b16), vm((ALLB, 3 * HD), b16), vm((BEA, 2 * HD), b16),
        vm((NX * BLK, REP * HD), b16), vm((NX * BLK, REP * HD), b16), vm((NX * BLK, REP * HD), b16),
        vm((NX, ROWS, HD), b16), vm((NX, ROWS, HD), b16),
        vm((1 + NX, ROWS, STEP), f32), vm((ROWS, HD), f32), vm((ROWS, 2 * HD), f32),
        vm((NX, 1, ROWS), f32), vm((NX, 1, ROWS), f32),
        vm((256, HD), f32), vm((256, HD), f32), vm((PLANE, 2 * BEA, HD), f32), vm((PLANE, 2 * BEA, HD), f32),
        vm((NG, 8, HD), f32), vm((NG, 8, HD), f32), vm((HD, HD), f32), vm((HD, HD), f32),
        dma((NG,)), dma((NG,)), dma((NG,)), dma((NG,)), dma((NG,)), dma((NG,)), dma((NG,)), dma((NG,)),
        dma((NX, 2)), dma((NX, 4)), dma((NX, 2)), dma((PLANE,)), dma((PLANE,)),
        dma((NG,)), dma((NG,)), dma((PLANE,)), dma((PLANE,)), dma((NG,)), dma((NG,)), dma((NG,)), dma((NG,)),
    ]
    anyspace = pl.BlockSpec(memory_space=pl.ANY)
    inner = pl.BlockSpec(memory_space=pltpu.VMEM)
    return pl.pallas_call(
        fused,
        out_shape=(
            jax.ShapeDtypeStruct((TOK, NG * REP * HD), b16),
            jax.ShapeDtypeStruct((4, NG * REP * HD), f32),
            jax.ShapeDtypeStruct((4, NG * HD), f32),
            jax.ShapeDtypeStruct((4, NG * HD), f32),
        ),
        in_specs=[anyspace] * 4,
        out_specs=(anyspace, inner, inner, inner),
        scratch_shapes=scratch,
        compiler_params=pltpu.CompilerParams(
            collective_id=0 if COMM else None, has_side_effects=True, vmem_limit_bytes=60 * 1024 * 1024
        ),
    )(query, key, value, d_out)


def solution(mesh):
    spec = P(("span", "ulysses"), None)
    return jax.shard_map(
        on_device, mesh=mesh, in_specs=(spec,) * 4, out_specs=(spec,) * 4, check_vma=False
    )
```

```python
import functools
import math

import jax
import jax.numpy as jnp
from jax import lax
from jax.experimental import pallas as pl
from jax.experimental.pallas import tpu as pltpu
from jax.sharding import PartitionSpec as P

NX, NZ, NC, NS = 4, 4, 2, 8
NG = NX * NC
HD = 128
REP = 4
TOK = 128
BLK = NC * TOK
STEP = NZ * BLK
LOC = NX * STEP
ROWS = REP * BLK
BEA = 32
BSP = BEA * NZ
ALLB = NS * BSP
PLANE = NS * NZ
SCALE = 1.0 / math.sqrt(HD)
LOG2E = 1.4426950408889634
C2 = SCALE * LOG2E
MESH = pl.DeviceIdType.MESH
COMM = True
FWD = True
BWD = True


def dot_t(a, b):
    return lax.dot_general(a, b, (((1,), (1,)), ((), ())), preferred_element_type=jnp.float32)


def dot_n(a, b):
    return lax.dot_general(a, b, (((1,), (0,)), ((), ())), preferred_element_type=jnp.float32)


def iota(shape, dim):
    return lax.broadcasted_iota(jnp.int32, shape, dim)


def fused(
    q_hbm, k_hbm, v_hbm, do_hbm,
    out_hbm, gq_ref, gk_ref, gv_ref,
    kv, kvb, bst, qg, dog, outg, q4, do4, sbuf, mx, acc, lse_row, del_row,
    dk_acc, dv_acc, gacc, slots, tiles, gkv_in, dq_st, gq_in,
    kx_s, kx_r, vx_s, vx_r, q_s, q_r, do_s, do_r, z_s, z_r, zr_s, b_s, b_r,
    o_s, o_r, g_s, g_r, t_s, t_r, d_s, d_r,
):
    c = lax.axis_index("span")
    u = lax.axis_index("ulysses")
    x = u // (NZ * NC)
    z = (u // NC) % NZ
    core = u % NC
    g = x * NC + core
    me = c * NZ + z
    zp, zm = (z + 1) % NZ, (z + NZ - 1) % NZ

    def uly(grp, zz):
        return (grp // NC) * (NZ * NC) + zz * NC + grp % NC

    def in_group(grp):
        return {"span": c, "ulysses": uly(grp, z)}

    def in_plane(s):
        return {"span": s // NZ, "ulysses": uly(g, s % NZ)}

    def remote(src, dst, ssem, rsem, dev):
        return pltpu.make_async_remote_copy(
            src_ref=src, dst_ref=dst, send_sem=ssem, recv_sem=rsem, device_id=dev, device_id_type=MESH
        )

    def arrived(dst, sem):
        pltpu.make_async_copy(dst, dst, sem).wait()

    def kv_rows(grp, zz):
        return pl.ds((grp // NC) * STEP + zz * BLK + (grp % NC) * TOK, TOK)

    def piece_k(grp):
        return kv.at[kv_rows(grp, z), pl.ds(0, HD)]

    def piece_v(grp):
        return kv.at[kv_rows(grp, z), pl.ds(HD, HD)]

    def piece_q(buf, grp):
        return buf.at[pl.ds(grp * TOK, TOK), :]

    def x_copies(to, src_k=True):
        cols = pl.ds(pl.multiple_of(to * HD, HD), HD)
        wide = pl.ds(pl.multiple_of(to * REP * HD, REP * HD), REP * HD)
        return (
            (k_hbm.at[:, cols], piece_k(g), kx_s.at[to], kx_r.at[g]),
            (v_hbm.at[:, cols], piece_v(g), vx_s.at[to], vx_r.at[g]),
            (q_hbm.at[:, wide], piece_q(qg, g), q_s.at[to], q_r.at[g]),
            (do_hbm.at[:, wide], piece_q(dog, g), do_s.at[to], do_r.at[g]),
        )

    def z_rows(xx, zz):
        return pl.ds(xx * STEP + zz * BLK, BLK)

    def z_piece(xx, zz, lo, width):
        return kv.at[z_rows(xx, zz), pl.ds(lo, width)]

    def z_dev(zz):
        return {"span": c, "ulysses": uly(g, zz)}

    def z_send(xx, way):
        to = zp if way == 0 else zm
        part = z_piece(xx, z, 0, 2 * HD)
        return remote(part, part, z_s.at[xx, way], z_r.at[xx, way], z_dev(to))

    def z_relay(xx, way):
        to, of = (zp, zm) if way == 0 else (zm, zp)
        part = z_piece(xx, of, way * HD, HD)
        return remote(part, part, zr_s.at[xx, way], z_r.at[xx, 2 + way], z_dev(to))

    def b_rows(s):
        return kvb.at[pl.ds(pl.multiple_of(s * BEA, BEA), BEA), pl.ds(0, 2 * HD)]

    def b_send(s):
        return remote(bst, b_rows(me), b_s.at[s], b_r.at[me], in_plane(s))

    def o_send(grp):
        dst = out_hbm.at[:, pl.ds(pl.multiple_of(g * REP * HD, REP * HD), REP * HD)]
        return remote(piece_q(outg, grp), dst, o_s.at[grp], o_r.at[g], in_group(grp))

    def g_send(s):
        return remote(gacc.at[s], slots.at[me], g_s.at[s], g_r.at[me], in_plane(s))

    def t_send(grp):
        return remote(tiles.at[grp], gkv_in.at[g], t_s.at[grp], t_r.at[g], in_group(grp))

    def d_send(grp):
        return remote(
            dq_st.at[pl.ds(pl.multiple_of(grp * 16, 16), 16), :],
            gq_in.at[pl.ds(pl.multiple_of(g * 16, 16), 16), :],
            d_s.at[grp], d_r.at[g], in_group(grp),
        )

    def others(body):
        for k in range(1, NG):
            body((g + k) % NG)

    def plane(lo, hi, body):
        def one(s, carry):
            @pl.when(s != me)
            def _():
                body(s)

            return carry

        lax.fori_loop(lo, hi, one, 0)

    if COMM:
        barrier = pltpu.get_barrier_semaphore()
        others(lambda grp: pl.semaphore_signal(barrier, inc=1, device_id=in_group(grp), device_id_type=MESH))
        plane(0, PLANE, lambda s: pl.semaphore_signal(barrier, inc=1, device_id=in_plane(s), device_id_type=MESH))
        pl.semaphore_wait(barrier, NG - 1 + PLANE - 1)

    mine = x_copies(g)
    for which in range(4):
        src, dst, _, rsem = mine[which]
        pltpu.make_async_copy(src, dst, rsem).start()
        if COMM:
            others(lambda grp, which=which: remote(*x_copies(grp)[which], in_group(grp)).start())

    kv[:, pl.ds(2 * HD, HD)] = jnp.ones((LOC, HD), jnp.bfloat16)
    kvb[:, pl.ds(2 * HD, HD)] = jnp.ones((ALLB, HD), jnp.bfloat16)

    def wait_group(buf_piece, sem, grp):
        arrived(buf_piece(grp), sem.at[grp])

    def kv_here(xx):
        for cc in range(NC):
            wait_group(piece_k, kx_r, xx * NC + cc)
            wait_group(piece_v, vx_r, xx * NC + cc)

    def z_direct(xx):
        z_send(xx, 0).start()
        z_send(xx, 1).start()

    def z_pass_on(xx):
        arrived(z_piece(xx, zm, 0, 2 * HD), z_r.at[xx, 0])
        z_relay(xx, 0).start()
        arrived(z_piece(xx, zp, 0, 2 * HD), z_r.at[xx, 1])
        z_relay(xx, 1).start()

    if COMM:
        kv_here(0)
        z_direct(0)
        kv_here(1)
        z_direct(1)
        kv_here(2)
        kv_here(3)
    else:
        wait_group(piece_k, kx_r, g)
        wait_group(piece_v, vx_r, g)

    picked = jnp.zeros((BEA, 2 * HD), jnp.float32)
    for xx in range(NX):
        row, col = iota((BEA, BLK), 0), iota((BEA, BLK), 1)
        hot = (row * 32 + 31 == col + xx * BLK).astype(jnp.bfloat16)
        picked = picked + dot_n(hot, kv[z_rows(xx, z), pl.ds(0, 2 * HD)])
    bst[...] = picked.astype(jnp.bfloat16)
    kvb[pl.ds(pl.multiple_of(me * BEA, BEA), BEA), pl.ds(0, 2 * HD)] = bst[...]
    dk_acc[...] = jnp.zeros((ALLB, HD), jnp.float32)
    dv_acc[...] = jnp.zeros((ALLB, HD), jnp.float32)
    n_prior = (c + 1) // 2
    n_back = (c + 2) // 2
    z2 = (z + 2) % NZ
    if COMM:
        plane(c * NZ, PLANE, lambda s: b_send(s).start())
        z_pass_on(0)
        z_direct(2)
        z_pass_on(1)
        z_direct(3)
        plane(0, (c + 1) * NZ, lambda s: arrived(b_rows(s), b_r.at[s]))

    own = iota((256, 1), 0)

    def block(i, carry):
        if COMM:
            @pl.when((i == 1) | (i == 2))
            def _():
                z_pass_on(i + 1)

            arrived(z_piece(i, z2, 0, HD), z_r.at[i, 2])
            arrived(z_piece(i, z2, HD, HD), z_r.at[i, 3])
        for cc in range(NC):
            grp = i * NC + cc
            if COMM:
                wait_group(functools.partial(piece_q, qg), q_r, grp)
            else:
                pl.when(grp == g)(lambda: wait_group(functools.partial(piece_q, qg), q_r, g))
        for h in range(REP):
            q4[i, pl.ds(h * BLK, BLK), :] = qg[pl.ds(i * BLK, BLK), pl.ds(h * HD, HD)]
        mx[...] = jnp.full((ROWS, HD), -jnp.inf, jnp.float32)

        def widest(s, rows):
            top = s[:, :HD]
            for t in range(1, s.shape[1] // HD):
                top = jnp.maximum(top, s[:, t * HD : (t + 1) * HD])
            mx[rows, :] = jnp.maximum(mx[rows, :], top)

        def score_prior(jp, cr):
            keys = kvb[pl.ds(pl.multiple_of(jp * 256, 256), 256), pl.ds(0, HD)]
            for h in range(REP):
                rows = pl.ds(h * BLK, BLK)
                s = dot_t(q4[i, rows, :], keys)
                s = jnp.where(iota(s.shape, 1) < c * BSP - jp * 256, s, -jnp.inf)
                sbuf[0, rows, pl.ds(pl.multiple_of(jp * 256, 256), 256)] = s
                widest(s, rows)
            return cr

        lax.fori_loop(0, n_prior, score_prior, 0)

        def score(j, masked):
            keys = kv[pl.ds(pl.multiple_of(j * STEP, STEP), STEP), pl.ds(0, HD)]
            for h in range(REP):
                rows = pl.ds(h * BLK, BLK)
                s = dot_t(q4[i, rows, :], keys)
                if masked:
                    s = jnp.where(iota(s.shape, 1) - iota(s.shape, 0) <= z * BLK, s, -jnp.inf)
                sbuf[1 + j, rows, :] = s
                widest(s, rows)

        def score_full(j, cr):
            score(j, False)
            return cr

        lax.fori_loop(0, i, score_full, 0)
        score(i, True)

        peak = jnp.max(mx[...], axis=1, keepdims=True) * C2
        mx[...] = jnp.broadcast_to(peak, (ROWS, HD))
        acc[...] = jnp.zeros((ROWS, 2 * HD), jnp.float32)

        def spread(s, rows):
            m = mx[rows, :]
            return jnp.concatenate(
                [jnp.exp2(s[:, t * HD : (t + 1) * HD] * C2 - m) for t in range(s.shape[1] // HD)], axis=1
            ).astype(jnp.bfloat16)

        def mix_prior(jp, cr):
            at = pl.ds(pl.multiple_of(jp * 256, 256), 256)
            vals = kvb[at, pl.ds(HD, 2 * HD)]
            for h in range(REP):
                rows = pl.ds(h * BLK, BLK)
                acc[rows, :] += dot_n(spread(sbuf[0, rows, at], rows), vals)
            return cr

        lax.fori_loop(0, n_prior, mix_prior, 0)

        def mix(j, cr):
            vals = kv[pl.ds(pl.multiple_of(j * STEP, STEP), STEP), pl.ds(HD, 2 * HD)]
            for h in range(REP):
                rows = pl.ds(h * BLK, BLK)
                acc[rows, :] += dot_n(spread(sbuf[1 + j, rows, :], rows), vals)
            return cr

        lax.fori_loop(0, i + 1, mix, 0)
        eye = iota((HD, HD), 0) == iota((HD, HD), 1)
        for h in range(REP):
            rows = pl.ds(h * BLK, BLK)
            total = acc[rows, pl.ds(HD, HD)]
            outg[pl.ds(i * BLK, BLK), pl.ds(h * HD, HD)] = (acc[rows, pl.ds(0, HD)] / total).astype(jnp.bfloat16)
            lse = mx[rows, :] + jnp.log2(total)
            for t in range(BLK // HD):
                part = jnp.where(eye, lse[t * HD : (t + 1) * HD], 0.0)
                lse_row[i, :, pl.ds(h * BLK + t * HD, HD)] = jnp.sum(part, axis=0, keepdims=True)
        for cc in range(NC):
            grp = i * NC + cc

            @pl.when(grp != g)
            def _():
                if COMM:
                    o_send(grp).start()

            @pl.when(grp == g)
            def _():
                cols = pl.ds(pl.multiple_of(g * REP * HD, REP * HD), REP * HD)
                pltpu.make_async_copy(piece_q(outg, g), out_hbm.at[:, cols], o_r.at[g]).start()

        for cc in range(NC):
            grp = i * NC + cc
            if COMM:
                wait_group(functools.partial(piece_q, dog), do_r, grp)
            else:
                pl.when(grp == g)(lambda: wait_group(functools.partial(piece_q, dog), do_r, g))
        eye = iota((HD, HD), 0) == iota((HD, HD), 1)
        for h in range(REP):
            cols = pl.ds(h * HD, HD)
            grad = dog[pl.ds(i * BLK, BLK), cols]
            do4[i, pl.ds(h * BLK, BLK), :] = grad
            prod = grad.astype(jnp.float32) * outg[pl.ds(i * BLK, BLK), cols].astype(jnp.float32)
            total = jnp.broadcast_to(jnp.sum(prod, axis=1, keepdims=True), prod.shape)
            for t in range(BLK // HD):
                part = jnp.where(eye, total[t * HD : (t + 1) * HD], 0.0)
                del_row[i, :, pl.ds(h * BLK + t * HD, HD)] = jnp.sum(part, axis=0, keepdims=True)

        def back(cp, cr):
            at = pl.ds(pl.multiple_of(cp * 256, 256), 256)
            rel = own + cp * 256 - c * BSP
            place = (rel % 32 // 8) * STEP + (rel // 32) * BLK + (rel % 8) * 32 + 31
            place = jnp.where(rel < 0, -1, jnp.where(rel >= BSP, LOC, place))
            keys, vals = kvb[at, pl.ds(0, HD)], kvb[at, pl.ds(HD, HD)]
            here = iota((1, ROWS), 1) % BLK + i * STEP + z * BLK
            p = jnp.where(place <= here, jnp.exp2(dot_t(keys, q4[i]) * C2 - lse_row[i]), 0.0)
            dp = dot_t(vals, do4[i])
            ds = (p * (dp - del_row[i])).astype(jnp.bfloat16)
            dv_acc[at, :] += dot_n(p.astype(jnp.bfloat16), do4[i])
            dk_acc[at, :] += dot_n(ds, q4[i])

            @pl.when(i == NX - 1)
            def _():
                for a in range(2):
                    for zz in range(NZ):
                        s = (cp * 2 + a) * NZ + zz
                        rows = pl.ds(pl.multiple_of(s * BEA, BEA), BEA)
                        gacc[s, pl.ds(0, BEA), :] = dk_acc[rows, :] * SCALE
                        gacc[s, pl.ds(BEA, BEA), :] = dv_acc[rows, :]
                if COMM:
                    plane(cp * 2 * NZ, jnp.minimum(cp * 2 + 2, c + 1) * NZ, lambda s: g_send(s).start())

            return cr

        if BWD:
            lax.fori_loop(0, n_back, back, 0)
        return carry

    lax.fori_loop(0, NX, block, 0)
    if BWD:
        row = iota((HD, 1), 0)
        dest, head, num = row // 16, (row // 4) % 4, row % 4
        spot = head * BLK + (dest % NC) * TOK + num * 32 + 31
        here = (dest // NC) * STEP + z * BLK + (dest % NC) * TOK + num * 32 + 31
        qb = jnp.zeros((HD, HD), jnp.float32)
        gb = jnp.zeros((HD, HD), jnp.float32)
        lse_b = jnp.zeros((HD, 1), jnp.float32)
        del_b = jnp.zeros((HD, 1), jnp.float32)
        for i in range(NX):
            pick = (iota((HD, ROWS), 1) == spot) & (dest // NC == i)
            hot = pick.astype(jnp.bfloat16)
            qb = qb + dot_n(hot, q4[i])
            gb = gb + dot_n(hot, do4[i])
            lse_b = lse_b + jnp.sum(jnp.where(pick, lse_row[i], 0.0), axis=1, keepdims=True)
            del_b = del_b + jnp.sum(jnp.where(pick, del_row[i], 0.0), axis=1, keepdims=True)
        qb = qb.astype(jnp.bfloat16)
        gb = gb.astype(jnp.bfloat16)

        def dq_part(keys, vals, seen):
            s = dot_t(qb, keys)
            p = jnp.where(seen(iota(s.shape, 1)), jnp.exp2(s * C2 - lse_b), 0.0)
            ds = (p * (dot_t(gb, vals) - del_b)).astype(jnp.bfloat16)
            return dot_n(ds, keys)

        def dq_prior(jp, total):
            at = pl.ds(pl.multiple_of(jp * 256, 256), 256)
            seen = lambda col: col < c * BSP - jp * 256
            return total + dq_part(kvb[at, pl.ds(0, HD)], kvb[at, pl.ds(HD, HD)], seen)

        dq = lax.fori_loop(0, n_prior, dq_prior, jnp.zeros((HD, HD), jnp.float32))

        def dq_local(j, total):
            at = pl.ds(pl.multiple_of(j * STEP, STEP), STEP)
            seen = lambda col: col + j * STEP <= here
            return total + dq_part(kv[at, pl.ds(0, HD)], kv[at, pl.ds(HD, HD)], seen)

        dq = lax.fori_loop(0, NX, dq_local, dq)
        dq_st[...] = dq * SCALE
    mine_rows = pl.ds(pl.multiple_of(g * 16, 16), 16)
    gq_in[mine_rows, :] = dq_st[mine_rows, :]
    if COMM:
        others(lambda grp: d_send(grp).start())

    dk_acc[pl.ds(0, 2 * BEA), :] = gacc[me]
    if COMM:

        def add(s):
            arrived(slots.at[s], g_r.at[s])
            dk_acc[pl.ds(0, 2 * BEA), :] += slots[s]

        plane(c * NZ, PLANE, add)
    for d in range(NG):
        tiles[d, pl.ds(0, 4), :] = dk_acc[pl.ds(d * 4, 4), :]
        tiles[d, pl.ds(4, 4), :] = dk_acc[pl.ds(BEA + d * 4, 4), :]
    gkv_in[g] = tiles[g]
    if COMM:
        others(lambda grp: t_send(grp).start())
        others(lambda grp: arrived(gq_in.at[pl.ds(pl.multiple_of(grp * 16, 16), 16), :], d_r.at[grp]))
        others(lambda grp: arrived(gkv_in.at[grp], t_r.at[grp]))
    for grp in range(NG):
        gk_ref[:, pl.ds(grp * HD, HD)] = gkv_in[grp, pl.ds(0, 4), :]
        gv_ref[:, pl.ds(grp * HD, HD)] = gkv_in[grp, pl.ds(4, 4), :]
        for h in range(REP):
            gq_ref[:, pl.ds((grp * REP + h) * HD, HD)] = gq_in[pl.ds(grp * 16 + h * 4, 4), :]

    def out_cols(grp):
        return out_hbm.at[:, pl.ds(pl.multiple_of(grp * REP * HD, REP * HD), REP * HD)]

    if FWD:
        arrived(out_cols(g), o_r.at[g])
    if COMM:
        others(lambda grp: arrived(out_cols(grp), o_r.at[grp]))
        for which in range(4):
            others(lambda grp, which=which: remote(*x_copies(grp)[which], in_group(grp)).wait_send())
        for xx in range(NX):
            for way in range(2):
                z_send(xx, way).wait_send()
                z_relay(xx, way).wait_send()
        plane(c * NZ, PLANE, lambda s: b_send(s).wait_send())
        others(lambda grp: o_send(grp).wait_send())
        plane(0, (c + 1) * NZ, lambda s: g_send(s).wait_send())
        others(lambda grp: d_send(grp).wait_send())
        others(lambda grp: t_send(grp).wait_send())


def on_device(query, key, value, d_out):
    f32, b16 = jnp.float32, jnp.bfloat16
    vm = pltpu.VMEM
    dma = pltpu.SemaphoreType.DMA
    scratch = [
        vm((LOC, 3 * HD), b16), vm((ALLB, 3 * HD), b16), vm((BEA, 2 * HD), b16),
        vm((NX * BLK, REP * HD), b16), vm((NX * BLK, REP * HD), b16), vm((NX * BLK, REP * HD), b16),
        vm((NX, ROWS, HD), b16), vm((NX, ROWS, HD), b16),
        vm((1 + NX, ROWS, STEP), f32), vm((ROWS, HD), f32), vm((ROWS, 2 * HD), f32),
        vm((NX, 1, ROWS), f32), vm((NX, 1, ROWS), f32),
        vm((ALLB, HD), f32), vm((ALLB, HD), f32), vm((PLANE, 2 * BEA, HD), f32), vm((PLANE, 2 * BEA, HD), f32),
        vm((NG, 8, HD), f32), vm((NG, 8, HD), f32), vm((HD, HD), f32), vm((HD, HD), f32),
        dma((NG,)), dma((NG,)), dma((NG,)), dma((NG,)), dma((NG,)), dma((NG,)), dma((NG,)), dma((NG,)),
        dma((NX, 2)), dma((NX, 4)), dma((NX, 2)), dma((PLANE,)), dma((PLANE,)),
        dma((NG,)), dma((NG,)), dma((PLANE,)), dma((PLANE,)), dma((NG,)), dma((NG,)), dma((NG,)), dma((NG,)),
    ]
    anyspace = pl.BlockSpec(memory_space=pl.ANY)
    inner = pl.BlockSpec(memory_space=pltpu.VMEM)
    return pl.pallas_call(
        fused,
        out_shape=(
            jax.ShapeDtypeStruct((TOK, NG * REP * HD), b16),
            jax.ShapeDtypeStruct((4, NG * REP * HD), f32),
            jax.ShapeDtypeStruct((4, NG * HD), f32),
            jax.ShapeDtypeStruct((4, NG * HD), f32),
        ),
        in_specs=[anyspace] * 4,
        out_specs=(anyspace, inner, inner, inner),
        scratch_shapes=scratch,
        compiler_params=pltpu.CompilerParams(
            collective_id=0 if COMM else None, has_side_effects=True, vmem_limit_bytes=60 * 1024 * 1024
        ),
    )(query, key, value, d_out)


def solution(mesh):
    spec = P(("span", "ulysses"), None)
    return jax.shard_map(
        on_device, mesh=mesh, in_specs=(spec,) * 4, out_specs=(spec,) * 4, check_vma=False
    )
```

```python
import functools
import math

import jax
import jax.numpy as jnp
from jax import lax
from jax.experimental import pallas as pl
from jax.experimental.pallas import tpu as pltpu
from jax.sharding import PartitionSpec as P

NX, NZ, NC, NS = 4, 4, 2, 8
NG = NX * NC
HD = 128
REP = 4
TOK = 128
BLK = NC * TOK
STEP = NZ * BLK
LOC = NX * STEP
ROWS = REP * BLK
BEA = 32
BSP = BEA * NZ
ALLB = NS * BSP
PLANE = NS * NZ
SCALE = 1.0 / math.sqrt(HD)
LOG2E = 1.4426950408889634
C2 = SCALE * LOG2E
MESH = pl.DeviceIdType.MESH
COMM = True
FWD = True
BWD = True


def dot_t(a, b):
    return lax.dot_general(a, b, (((1,), (1,)), ((), ())), preferred_element_type=jnp.float32)


def dot_n(a, b):
    return lax.dot_general(a, b, (((1,), (0,)), ((), ())), preferred_element_type=jnp.float32)


def iota(shape, dim):
    return lax.broadcasted_iota(jnp.int32, shape, dim)


def fused(
    q_hbm, k_hbm, v_hbm, do_hbm,
    out_hbm, gq_ref, gk_ref, gv_ref,
    kv, kvb, bst, qg, dog, outg, q4, do4, sbuf, mx, acc, lse_row, del_row,
    dk_acc, dv_acc, pb, dsb, gown, gacc, slots, tiles, gkv_in, dq_st, gq_in,
    kx_s, kx_r, vx_s, vx_r, q_s, q_r, do_s, do_r, z_s, z_r, zr_s, b_s, b_r,
    o_s, o_r, g_s, g_r, t_s, t_r, d_s, d_r,
):
    c = lax.axis_index("span")
    u = lax.axis_index("ulysses")
    x = u // (NZ * NC)
    z = (u // NC) % NZ
    core = u % NC
    g = x * NC + core
    me = c * NZ + z
    zp, zm = (z + 1) % NZ, (z + NZ - 1) % NZ

    def uly(grp, zz):
        return (grp // NC) * (NZ * NC) + zz * NC + grp % NC

    def in_group(grp):
        return {"span": c, "ulysses": uly(grp, z)}

    def in_plane(s):
        return {"span": s // NZ, "ulysses": uly(g, s % NZ)}

    def remote(src, dst, ssem, rsem, dev):
        return pltpu.make_async_remote_copy(
            src_ref=src, dst_ref=dst, send_sem=ssem, recv_sem=rsem, device_id=dev, device_id_type=MESH
        )

    def arrived(dst, sem):
        pltpu.make_async_copy(dst, dst, sem).wait()

    def kv_rows(grp, zz):
        return pl.ds((grp // NC) * STEP + zz * BLK + (grp % NC) * TOK, TOK)

    def piece_k(grp):
        return kv.at[kv_rows(grp, z), pl.ds(0, HD)]

    def piece_v(grp):
        return kv.at[kv_rows(grp, z), pl.ds(HD, HD)]

    def piece_q(buf, grp):
        return buf.at[pl.ds(grp * TOK, TOK), :]

    def x_copies(to, src_k=True):
        cols = pl.ds(pl.multiple_of(to * HD, HD), HD)
        wide = pl.ds(pl.multiple_of(to * REP * HD, REP * HD), REP * HD)
        return (
            (k_hbm.at[:, cols], piece_k(g), kx_s.at[to], kx_r.at[g]),
            (v_hbm.at[:, cols], piece_v(g), vx_s.at[to], vx_r.at[g]),
            (q_hbm.at[:, wide], piece_q(qg, g), q_s.at[to], q_r.at[g]),
            (do_hbm.at[:, wide], piece_q(dog, g), do_s.at[to], do_r.at[g]),
        )

    def z_rows(xx, zz):
        return pl.ds(xx * STEP + zz * BLK, BLK)

    def z_piece(xx, zz, lo, width):
        return kv.at[z_rows(xx, zz), pl.ds(lo, width)]

    def z_dev(zz):
        return {"span": c, "ulysses": uly(g, zz)}

    def z_send(xx, way):
        to = zp if way == 0 else zm
        part = z_piece(xx, z, 0, 2 * HD)
        return remote(part, part, z_s.at[xx, way], z_r.at[xx, way], z_dev(to))

    def z_relay(xx, way):
        to, of = (zp, zm) if way == 0 else (zm, zp)
        part = z_piece(xx, of, way * HD, HD)
        return remote(part, part, zr_s.at[xx, way], z_r.at[xx, 2 + way], z_dev(to))

    def b_rows(s):
        return kvb.at[pl.ds(pl.multiple_of(s * BEA, BEA), BEA), pl.ds(0, 2 * HD)]

    def b_send(s):
        return remote(bst, b_rows(me), b_s.at[s], b_r.at[me], in_plane(s))

    def o_send(grp):
        dst = out_hbm.at[:, pl.ds(pl.multiple_of(g * REP * HD, REP * HD), REP * HD)]
        return remote(piece_q(outg, grp), dst, o_s.at[grp], o_r.at[g], in_group(grp))

    def g_send(s):
        return remote(gacc.at[s], slots.at[me], g_s.at[s], g_r.at[me], in_plane(s))

    def t_send(grp):
        return remote(tiles.at[grp], gkv_in.at[g], t_s.at[grp], t_r.at[g], in_group(grp))

    def d_send(grp):
        return remote(
            dq_st.at[pl.ds(pl.multiple_of(grp * 16, 16), 16), :],
            gq_in.at[pl.ds(pl.multiple_of(g * 16, 16), 16), :],
            d_s.at[grp], d_r.at[g], in_group(grp),
        )

    def others(body):
        for k in range(1, NG):
            body((g + k) % NG)

    def plane(lo, hi, body):
        def one(s, carry):
            @pl.when(s != me)
            def _():
                body(s)

            return carry

        lax.fori_loop(lo, hi, one, 0)

    if COMM:
        barrier = pltpu.get_barrier_semaphore()
        others(lambda grp: pl.semaphore_signal(barrier, inc=1, device_id=in_group(grp), device_id_type=MESH))
        plane(0, PLANE, lambda s: pl.semaphore_signal(barrier, inc=1, device_id=in_plane(s), device_id_type=MESH))
        pl.semaphore_wait(barrier, NG - 1 + PLANE - 1)

    mine = x_copies(g)
    for which in range(4):
        src, dst, _, rsem = mine[which]
        pltpu.make_async_copy(src, dst, rsem).start()
        if COMM:
            others(lambda grp, which=which: remote(*x_copies(grp)[which], in_group(grp)).start())

    kv[:, pl.ds(2 * HD, HD)] = jnp.ones((LOC, HD), jnp.bfloat16)
    kvb[:, pl.ds(2 * HD, HD)] = jnp.ones((ALLB, HD), jnp.bfloat16)

    def wait_group(buf_piece, sem, grp):
        arrived(buf_piece(grp), sem.at[grp])

    def kv_here(xx):
        for cc in range(NC):
            wait_group(piece_k, kx_r, xx * NC + cc)
            wait_group(piece_v, vx_r, xx * NC + cc)

    def z_direct(xx):
        z_send(xx, 0).start()
        z_send(xx, 1).start()

    def z_pass_on(xx):
        arrived(z_piece(xx, zm, 0, 2 * HD), z_r.at[xx, 0])
        z_relay(xx, 0).start()
        arrived(z_piece(xx, zp, 0, 2 * HD), z_r.at[xx, 1])
        z_relay(xx, 1).start()

    if COMM:
        kv_here(0)
        z_direct(0)
        kv_here(1)
        z_direct(1)
        kv_here(2)
        kv_here(3)
    else:
        wait_group(piece_k, kx_r, g)
        wait_group(piece_v, vx_r, g)

    picked = jnp.zeros((BEA, 2 * HD), jnp.float32)
    for xx in range(NX):
        row, col = iota((BEA, BLK), 0), iota((BEA, BLK), 1)
        hot = (row * 32 + 31 == col + xx * BLK).astype(jnp.bfloat16)
        picked = picked + dot_n(hot, kv[z_rows(xx, z), pl.ds(0, 2 * HD)])
    bst[...] = picked.astype(jnp.bfloat16)
    kvb[pl.ds(pl.multiple_of(me * BEA, BEA), BEA), pl.ds(0, 2 * HD)] = bst[...]
    n_prior = (c + 1) // 2
    n_back = (c + 2) // 2
    z2 = (z + 2) % NZ
    if COMM:
        plane(c * NZ, PLANE, lambda s: b_send(s).start())
        z_pass_on(0)
        z_direct(2)
        z_pass_on(1)
        z_direct(3)
        plane(0, (c + 1) * NZ, lambda s: arrived(b_rows(s), b_r.at[s]))

    own = iota((256, 1), 0)

    def block(i, carry):
        if COMM:
            @pl.when((i == 1) | (i == 2))
            def _():
                z_pass_on(i + 1)

            arrived(z_piece(i, z2, 0, HD), z_r.at[i, 2])
            arrived(z_piece(i, z2, HD, HD), z_r.at[i, 3])
        for cc in range(NC):
            grp = i * NC + cc
            if COMM:
                wait_group(functools.partial(piece_q, qg), q_r, grp)
            else:
                pl.when(grp == g)(lambda: wait_group(functools.partial(piece_q, qg), q_r, g))
        for h in range(REP):
            q4[i, pl.ds(h * BLK, BLK), :] = qg[pl.ds(i * BLK, BLK), pl.ds(h * HD, HD)]
        mx[...] = jnp.full((ROWS, HD), -jnp.inf, jnp.float32)

        def widest(s, rows):
            top = s[:, :HD]
            for t in range(1, s.shape[1] // HD):
                top = jnp.maximum(top, s[:, t * HD : (t + 1) * HD])
            mx[rows, :] = jnp.maximum(mx[rows, :], top)

        def score_prior(jp, cr):
            keys = kvb[pl.ds(pl.multiple_of(jp * 256, 256), 256), pl.ds(0, HD)]
            for h in range(REP):
                rows = pl.ds(h * BLK, BLK)
                s = dot_t(q4[i, rows, :], keys)
                s = jnp.where(iota(s.shape, 1) < c * BSP - jp * 256, s, -jnp.inf)
                sbuf[0, rows, pl.ds(pl.multiple_of(jp * 256, 256), 256)] = s
                widest(s, rows)
            return cr

        lax.fori_loop(0, n_prior, score_prior, 0)

        def score(j, masked):
            keys = kv[pl.ds(pl.multiple_of(j * STEP, STEP), STEP), pl.ds(0, HD)]
            for h in range(REP):
                rows = pl.ds(h * BLK, BLK)
                s = dot_t(q4[i, rows, :], keys)
                if masked:
                    s = jnp.where(iota(s.shape, 1) - iota(s.shape, 0) <= z * BLK, s, -jnp.inf)
                sbuf[1 + j, rows, :] = s
                widest(s, rows)

        def score_full(j, cr):
            score(j, False)
            return cr

        lax.fori_loop(0, i, score_full, 0)
        score(i, True)

        peak = jnp.max(mx[...], axis=1, keepdims=True) * C2
        mx[...] = jnp.broadcast_to(peak, (ROWS, HD))
        acc[...] = jnp.zeros((ROWS, 2 * HD), jnp.float32)

        def spread(s, rows):
            m = mx[rows, :]
            return jnp.concatenate(
                [jnp.exp2(s[:, t * HD : (t + 1) * HD] * C2 - m) for t in range(s.shape[1] // HD)], axis=1
            ).astype(jnp.bfloat16)

        def mix_prior(jp, cr):
            at = pl.ds(pl.multiple_of(jp * 256, 256), 256)
            vals = kvb[at, pl.ds(HD, 2 * HD)]
            for h in range(REP):
                rows = pl.ds(h * BLK, BLK)
                acc[rows, :] += dot_n(spread(sbuf[0, rows, at], rows), vals)
            return cr

        lax.fori_loop(0, n_prior, mix_prior, 0)

        def mix(j, cr):
            vals = kv[pl.ds(pl.multiple_of(j * STEP, STEP), STEP), pl.ds(HD, 2 * HD)]
            for h in range(REP):
                rows = pl.ds(h * BLK, BLK)
                acc[rows, :] += dot_n(spread(sbuf[1 + j, rows, :], rows), vals)
            return cr

        lax.fori_loop(0, i + 1, mix, 0)
        eye = iota((HD, HD), 0) == iota((HD, HD), 1)
        for h in range(REP):
            rows = pl.ds(h * BLK, BLK)
            total = acc[rows, pl.ds(HD, HD)]
            outg[pl.ds(i * BLK, BLK), pl.ds(h * HD, HD)] = (acc[rows, pl.ds(0, HD)] / total).astype(jnp.bfloat16)
            lse = mx[rows, :] + jnp.log2(total)
            for t in range(BLK // HD):
                part = jnp.where(eye, lse[t * HD : (t + 1) * HD], 0.0)
                lse_row[i, :, pl.ds(h * BLK + t * HD, HD)] = jnp.sum(part, axis=0, keepdims=True)
        for cc in range(NC):
            grp = i * NC + cc

            @pl.when(grp != g)
            def _():
                if COMM:
                    o_send(grp).start()

            @pl.when(grp == g)
            def _():
                cols = pl.ds(pl.multiple_of(g * REP * HD, REP * HD), REP * HD)
                pltpu.make_async_copy(piece_q(outg, g), out_hbm.at[:, cols], o_r.at[g]).start()

        for cc in range(NC):
            grp = i * NC + cc
            if COMM:
                wait_group(functools.partial(piece_q, dog), do_r, grp)
            else:
                pl.when(grp == g)(lambda: wait_group(functools.partial(piece_q, dog), do_r, g))
        eye = iota((HD, HD), 0) == iota((HD, HD), 1)
        for h in range(REP):
            cols = pl.ds(h * HD, HD)
            grad = dog[pl.ds(i * BLK, BLK), cols]
            do4[i, pl.ds(h * BLK, BLK), :] = grad
            prod = grad.astype(jnp.float32) * outg[pl.ds(i * BLK, BLK), cols].astype(jnp.float32)
            total = jnp.broadcast_to(jnp.sum(prod, axis=1, keepdims=True), prod.shape)
            for t in range(BLK // HD):
                part = jnp.where(eye, total[t * HD : (t + 1) * HD], 0.0)
                del_row[i, :, pl.ds(h * BLK + t * HD, HD)] = jnp.sum(part, axis=0, keepdims=True)

        return carry

    lax.fori_loop(0, NX, block, 0)

    def back(cp, carry):
        at = pl.ds(pl.multiple_of(cp * 256, 256), 256)
        rel = own + cp * 256 - c * BSP
        place = (rel % 32 // 8) * STEP + (rel // 32) * BLK + (rel % 8) * 32 + 31
        place = jnp.where(rel < 0, -1, jnp.where(rel >= BSP, LOC, place))
        keys, vals = kvb[at, pl.ds(0, HD)], kvb[at, pl.ds(HD, HD)]
        dk_acc[...] = jnp.zeros((256, HD), jnp.float32)
        dv_acc[...] = jnp.zeros((256, HD), jnp.float32)

        def one(i, cr):
            for h in range(REP):
                rows = pl.ds(h * BLK, BLK)
                qs, gs = q4[i, rows, :], do4[i, rows, :]
                here = iota((1, BLK), 1) + i * STEP + z * BLK
                p = jnp.where(place <= here, jnp.exp2(dot_t(keys, qs) * C2 - lse_row[i, :, rows]), 0.0)
                dsb[:, rows] = (p * (dot_t(vals, gs) - del_row[i, :, rows])).astype(jnp.bfloat16)
                pb[:, rows] = p.astype(jnp.bfloat16)
            dv_acc[...] += dot_n(pb[...], do4[i])
            dk_acc[...] += dot_n(dsb[...], q4[i])
            return cr

        lax.fori_loop(0, NX, one, 0)
        for a in range(2):
            for zz in range(NZ):
                s = (cp * 2 + a) * NZ + zz
                rows = pl.ds(a * BSP + zz * BEA, BEA)
                gacc[s, pl.ds(0, BEA), :] = (dk_acc[rows, :] * SCALE).astype(jnp.bfloat16)
                gacc[s, pl.ds(BEA, BEA), :] = dv_acc[rows, :].astype(jnp.bfloat16)

                @pl.when(s == me)
                def _():
                    gown[pl.ds(0, BEA), :] = dk_acc[rows, :] * SCALE
                    gown[pl.ds(BEA, BEA), :] = dv_acc[rows, :]

        if COMM:
            plane(cp * 2 * NZ, jnp.minimum(cp * 2 + 2, c + 1) * NZ, lambda s: g_send(s).start())
        return carry

    if BWD:
        lax.fori_loop(0, n_back, back, 0)

        row = iota((HD, 1), 0)
        dest, head, num = row // 16, (row // 4) % 4, row % 4
        spot = head * BLK + (dest % NC) * TOK + num * 32 + 31
        here = (dest // NC) * STEP + z * BLK + (dest % NC) * TOK + num * 32 + 31
        qb = jnp.zeros((HD, HD), jnp.float32)
        gb = jnp.zeros((HD, HD), jnp.float32)
        lse_b = jnp.zeros((HD, 1), jnp.float32)
        del_b = jnp.zeros((HD, 1), jnp.float32)
        for i in range(NX):
            pick = (iota((HD, ROWS), 1) == spot) & (dest // NC == i)
            hot = pick.astype(jnp.bfloat16)
            qb = qb + dot_n(hot, q4[i])
            gb = gb + dot_n(hot, do4[i])
            lse_b = lse_b + jnp.sum(jnp.where(pick, lse_row[i], 0.0), axis=1, keepdims=True)
            del_b = del_b + jnp.sum(jnp.where(pick, del_row[i], 0.0), axis=1, keepdims=True)
        qb = qb.astype(jnp.bfloat16)
        gb = gb.astype(jnp.bfloat16)

        def dq_part(keys, vals, seen):
            s = dot_t(qb, keys)
            p = jnp.where(seen(iota(s.shape, 1)), jnp.exp2(s * C2 - lse_b), 0.0)
            ds = (p * (dot_t(gb, vals) - del_b)).astype(jnp.bfloat16)
            return dot_n(ds, keys)

        def dq_prior(jp, total):
            at = pl.ds(pl.multiple_of(jp * 256, 256), 256)
            seen = lambda col: col < c * BSP - jp * 256
            return total + dq_part(kvb[at, pl.ds(0, HD)], kvb[at, pl.ds(HD, HD)], seen)

        dq = lax.fori_loop(0, n_prior, dq_prior, jnp.zeros((HD, HD), jnp.float32))

        def dq_local(j, total):
            at = pl.ds(pl.multiple_of(j * STEP, STEP), STEP)
            seen = lambda col: col + j * STEP <= here
            return total + dq_part(kv[at, pl.ds(0, HD)], kv[at, pl.ds(HD, HD)], seen)

        dq = lax.fori_loop(0, NX, dq_local, dq)
        dq_st[...] = dq * SCALE
    mine_rows = pl.ds(pl.multiple_of(g * 16, 16), 16)
    gq_in[mine_rows, :] = dq_st[mine_rows, :]
    if COMM:
        others(lambda grp: d_send(grp).start())

    if COMM:

        def add(s):
            arrived(slots.at[s], g_r.at[s])
            gown[...] += slots[s].astype(jnp.float32)

        plane(c * NZ, PLANE, add)
    for d in range(NG):
        tiles[d, pl.ds(0, 4), :] = gown[pl.ds(d * 4, 4), :]
        tiles[d, pl.ds(4, 4), :] = gown[pl.ds(BEA + d * 4, 4), :]
    gkv_in[g] = tiles[g]
    if COMM:
        others(lambda grp: t_send(grp).start())
        others(lambda grp: arrived(gq_in.at[pl.ds(pl.multiple_of(grp * 16, 16), 16), :], d_r.at[grp]))
        others(lambda grp: arrived(gkv_in.at[grp], t_r.at[grp]))
    for grp in range(NG):
        gk_ref[:, pl.ds(grp * HD, HD)] = gkv_in[grp, pl.ds(0, 4), :]
        gv_ref[:, pl.ds(grp * HD, HD)] = gkv_in[grp, pl.ds(4, 4), :]
        for h in range(REP):
            gq_ref[:, pl.ds((grp * REP + h) * HD, HD)] = gq_in[pl.ds(grp * 16 + h * 4, 4), :]

    def out_cols(grp):
        return out_hbm.at[:, pl.ds(pl.multiple_of(grp * REP * HD, REP * HD), REP * HD)]

    if FWD:
        arrived(out_cols(g), o_r.at[g])
    if COMM:
        others(lambda grp: arrived(out_cols(grp), o_r.at[grp]))
        for which in range(4):
            others(lambda grp, which=which: remote(*x_copies(grp)[which], in_group(grp)).wait_send())
        for xx in range(NX):
            for way in range(2):
                z_send(xx, way).wait_send()
                z_relay(xx, way).wait_send()
        plane(c * NZ, PLANE, lambda s: b_send(s).wait_send())
        others(lambda grp: o_send(grp).wait_send())
        plane(0, (c + 1) * NZ, lambda s: g_send(s).wait_send())
        others(lambda grp: d_send(grp).wait_send())
        others(lambda grp: t_send(grp).wait_send())


def on_device(query, key, value, d_out):
    f32, b16 = jnp.float32, jnp.bfloat16
    vm = pltpu.VMEM
    dma = pltpu.SemaphoreType.DMA
    scratch = [
        vm((LOC, 3 * HD), b16), vm((ALLB, 3 * HD), b16), vm((BEA, 2 * HD), b16),
        vm((NX * BLK, REP * HD), b16), vm((NX * BLK, REP * HD), b16), vm((NX * BLK, REP * HD), b16),
        vm((NX, ROWS, HD), b16), vm((NX, ROWS, HD), b16),
        vm((1 + NX, ROWS, STEP), f32), vm((ROWS, HD), f32), vm((ROWS, 2 * HD), f32),
        vm((NX, 1, ROWS), f32), vm((NX, 1, ROWS), f32),
        vm((256, HD), f32), vm((256, HD), f32), vm((256, ROWS), b16), vm((256, ROWS), b16), vm((2 * BEA, HD), f32), vm((PLANE, 2 * BEA, HD), b16), vm((PLANE, 2 * BEA, HD), b16),
        vm((NG, 8, HD), f32), vm((NG, 8, HD), f32), vm((HD, HD), f32), vm((HD, HD), f32),
        dma((NG,)), dma((NG,)), dma((NG,)), dma((NG,)), dma((NG,)), dma((NG,)), dma((NG,)), dma((NG,)),
        dma((NX, 2)), dma((NX, 4)), dma((NX, 2)), dma((PLANE,)), dma((PLANE,)),
        dma((NG,)), dma((NG,)), dma((PLANE,)), dma((PLANE,)), dma((NG,)), dma((NG,)), dma((NG,)), dma((NG,)),
    ]
    anyspace = pl.BlockSpec(memory_space=pl.ANY)
    inner = pl.BlockSpec(memory_space=pltpu.VMEM)
    return pl.pallas_call(
        fused,
        out_shape=(
            jax.ShapeDtypeStruct((TOK, NG * REP * HD), b16),
            jax.ShapeDtypeStruct((4, NG * REP * HD), f32),
            jax.ShapeDtypeStruct((4, NG * HD), f32),
            jax.ShapeDtypeStruct((4, NG * HD), f32),
        ),
        in_specs=[anyspace] * 4,
        out_specs=(anyspace, inner, inner, inner),
        scratch_shapes=scratch,
        compiler_params=pltpu.CompilerParams(
            collective_id=0 if COMM else None, has_side_effects=True, vmem_limit_bytes=60 * 1024 * 1024
        ),
    )(query, key, value, d_out)


def solution(mesh):
    spec = P(("span", "ulysses"), None)
    return jax.shard_map(
        on_device, mesh=mesh, in_specs=(spec,) * 4, out_specs=(spec,) * 4, check_vma=False
    )
```

```python
import functools
import math

import jax
import jax.numpy as jnp
from jax import lax
from jax.experimental import pallas as pl
from jax.experimental.pallas import tpu as pltpu
from jax.sharding import PartitionSpec as P

NX, NZ, NC, NS = 4, 4, 2, 8
NG = NX * NC
HD = 128
REP = 4
TOK = 128
BLK = NC * TOK
STEP = NZ * BLK
LOC = NX * STEP
ROWS = REP * BLK
BEA = 32
BSP = BEA * NZ
ALLB = NS * BSP
PLANE = NS * NZ
SCALE = 1.0 / math.sqrt(HD)
LOG2E = 1.4426950408889634
C2 = SCALE * LOG2E
MESH = pl.DeviceIdType.MESH
PCH = 1024
COMM = True
FWD = True
BWD = True


def dot_t(a, b):
    return lax.dot_general(a, b, (((1,), (1,)), ((), ())), preferred_element_type=jnp.float32)


def dot_n(a, b):
    return lax.dot_general(a, b, (((1,), (0,)), ((), ())), preferred_element_type=jnp.float32)


def iota(shape, dim):
    return lax.broadcasted_iota(jnp.int32, shape, dim)


def fused(
    q_hbm, k_hbm, v_hbm, do_hbm,
    out_hbm, gq_ref, gk_ref, gv_ref,
    kv, kvb, bst, qg, dog, outg, q4, do4, sbuf, mx, acc, lse_row, del_row,
    dk_acc, dv_acc, pb, dsb, gown, gacc, slots, tiles, gkv_in, dq_st, gq_in,
    kx_s, kx_r, vx_s, vx_r, q_s, q_r, do_s, do_r, z_s, z_r, zr_s, b_s, b_r,
    o_s, o_r, g_s, g_r, t_s, t_r, d_s, d_r,
):
    c = lax.axis_index("span")
    u = lax.axis_index("ulysses")
    x = u // (NZ * NC)
    z = (u // NC) % NZ
    core = u % NC
    g = x * NC + core
    me = c * NZ + z
    zp, zm = (z + 1) % NZ, (z + NZ - 1) % NZ

    def uly(grp, zz):
        return (grp // NC) * (NZ * NC) + zz * NC + grp % NC

    def in_group(grp):
        return {"span": c, "ulysses": uly(grp, z)}

    def in_plane(s):
        return {"span": s // NZ, "ulysses": uly(g, s % NZ)}

    def remote(src, dst, ssem, rsem, dev):
        return pltpu.make_async_remote_copy(
            src_ref=src, dst_ref=dst, send_sem=ssem, recv_sem=rsem, device_id=dev, device_id_type=MESH
        )

    def arrived(dst, sem):
        pltpu.make_async_copy(dst, dst, sem).wait()

    def kv_rows(grp, zz):
        return pl.ds((grp // NC) * STEP + zz * BLK + (grp % NC) * TOK, TOK)

    def piece_k(grp):
        return kv.at[kv_rows(grp, z), pl.ds(0, HD)]

    def piece_v(grp):
        return kv.at[kv_rows(grp, z), pl.ds(HD, HD)]

    def piece_q(buf, grp):
        return buf.at[pl.ds(grp * TOK, TOK), :]

    def x_copies(to, src_k=True):
        cols = pl.ds(pl.multiple_of(to * HD, HD), HD)
        wide = pl.ds(pl.multiple_of(to * REP * HD, REP * HD), REP * HD)
        return (
            (k_hbm.at[:, cols], piece_k(g), kx_s.at[to], kx_r.at[g]),
            (v_hbm.at[:, cols], piece_v(g), vx_s.at[to], vx_r.at[g]),
            (q_hbm.at[:, wide], piece_q(qg, g), q_s.at[to], q_r.at[g]),
            (do_hbm.at[:, wide], piece_q(dog, g), do_s.at[to], do_r.at[g]),
        )

    def z_rows(xx, zz):
        return pl.ds(xx * STEP + zz * BLK, BLK)

    def z_piece(xx, zz, lo, width):
        return kv.at[z_rows(xx, zz), pl.ds(lo, width)]

    def z_dev(zz):
        return {"span": c, "ulysses": uly(g, zz)}

    def z_send(xx, way):
        to = zp if way == 0 else zm
        part = z_piece(xx, z, 0, 2 * HD)
        return remote(part, part, z_s.at[xx, way], z_r.at[xx, way], z_dev(to))

    def z_relay(xx, way):
        to, of = (zp, zm) if way == 0 else (zm, zp)
        part = z_piece(xx, of, way * HD, HD)
        return remote(part, part, zr_s.at[xx, way], z_r.at[xx, 2 + way], z_dev(to))

    def b_rows(s):
        return kvb.at[pl.ds(pl.multiple_of(s * BEA, BEA), BEA), pl.ds(0, 2 * HD)]

    def b_send(s):
        return remote(bst, b_rows(me), b_s.at[s], b_r.at[me], in_plane(s))

    def o_send(grp):
        dst = out_hbm.at[:, pl.ds(pl.multiple_of(g * REP * HD, REP * HD), REP * HD)]
        return remote(piece_q(outg, grp), dst, o_s.at[grp], o_r.at[g], in_group(grp))

    def g_send(s):
        return remote(gacc.at[s], slots.at[me], g_s.at[s], g_r.at[me], in_plane(s))

    def t_send(grp):
        return remote(tiles.at[grp], gkv_in.at[g], t_s.at[grp], t_r.at[g], in_group(grp))

    def d_send(grp):
        return remote(
            dq_st.at[pl.ds(pl.multiple_of(grp * 16, 16), 16), :],
            gq_in.at[pl.ds(pl.multiple_of(g * 16, 16), 16), :],
            d_s.at[grp], d_r.at[g], in_group(grp),
        )

    def others(body):
        for k in range(1, NG):
            body((g + k) % NG)

    def plane(lo, hi, body):
        def one(s, carry):
            @pl.when(s != me)
            def _():
                body(s)

            return carry

        lax.fori_loop(lo, hi, one, 0)

    if COMM:
        barrier = pltpu.get_barrier_semaphore()
        others(lambda grp: pl.semaphore_signal(barrier, inc=1, device_id=in_group(grp), device_id_type=MESH))
        plane(0, PLANE, lambda s: pl.semaphore_signal(barrier, inc=1, device_id=in_plane(s), device_id_type=MESH))
        pl.semaphore_wait(barrier, NG - 1 + PLANE - 1)

    mine = x_copies(g)
    for which in range(4):
        src, dst, _, rsem = mine[which]
        pltpu.make_async_copy(src, dst, rsem).start()
        if COMM:
            others(lambda grp, which=which: remote(*x_copies(grp)[which], in_group(grp)).start())

    kv[:, pl.ds(2 * HD, HD)] = jnp.ones((LOC, HD), jnp.bfloat16)
    kvb[:, pl.ds(2 * HD, HD)] = jnp.ones((ALLB, HD), jnp.bfloat16)

    def wait_group(buf_piece, sem, grp):
        arrived(buf_piece(grp), sem.at[grp])

    def kv_here(xx):
        for cc in range(NC):
            wait_group(piece_k, kx_r, xx * NC + cc)
            wait_group(piece_v, vx_r, xx * NC + cc)

    def z_direct(xx):
        z_send(xx, 0).start()
        z_send(xx, 1).start()

    def z_pass_on(xx):
        arrived(z_piece(xx, zm, 0, 2 * HD), z_r.at[xx, 0])
        z_relay(xx, 0).start()
        arrived(z_piece(xx, zp, 0, 2 * HD), z_r.at[xx, 1])
        z_relay(xx, 1).start()

    if COMM:
        kv_here(0)
        z_direct(0)
        kv_here(1)
        z_direct(1)
        kv_here(2)
        kv_here(3)
    else:
        wait_group(piece_k, kx_r, g)
        wait_group(piece_v, vx_r, g)

    picked = jnp.zeros((BEA, 2 * HD), jnp.float32)
    for xx in range(NX):
        row, col = iota((BEA, BLK), 0), iota((BEA, BLK), 1)
        hot = (row * 32 + 31 == col + xx * BLK).astype(jnp.bfloat16)
        picked = picked + dot_n(hot, kv[z_rows(xx, z), pl.ds(0, 2 * HD)])
    bst[...] = picked.astype(jnp.bfloat16)
    kvb[pl.ds(pl.multiple_of(me * BEA, BEA), BEA), pl.ds(0, 2 * HD)] = bst[...]
    n_prior = (c + 1) // 2
    n_chunk = (c * BSP + PCH - 1) // PCH
    n_back = (c + 2) // 2
    z2 = (z + 2) % NZ
    if COMM:
        plane(c * NZ, PLANE, lambda s: b_send(s).start())
        z_pass_on(0)
        z_direct(2)
        z_pass_on(1)
        z_direct(3)
        plane(0, (c + 1) * NZ, lambda s: arrived(b_rows(s), b_r.at[s]))

    own = iota((256, 1), 0)

    def blank(s, carry):
        kvb[pl.ds(pl.multiple_of(s * BSP, BSP), BSP), pl.ds(0, 2 * HD)] = jnp.zeros((BSP, 2 * HD), jnp.bfloat16)
        return carry

    lax.fori_loop(c + 1, NS, blank, 0)

    def block(i, carry):
        if COMM:
            @pl.when((i == 1) | (i == 2))
            def _():
                z_pass_on(i + 1)

            arrived(z_piece(i, z2, 0, HD), z_r.at[i, 2])
            arrived(z_piece(i, z2, HD, HD), z_r.at[i, 3])
        for cc in range(NC):
            grp = i * NC + cc
            if COMM:
                wait_group(functools.partial(piece_q, qg), q_r, grp)
            else:
                pl.when(grp == g)(lambda: wait_group(functools.partial(piece_q, qg), q_r, g))
        for h in range(REP):
            q4[i, pl.ds(h * BLK, BLK), :] = qg[pl.ds(i * BLK, BLK), pl.ds(h * HD, HD)]
        mx[...] = jnp.full((ROWS, HD), -jnp.inf, jnp.float32)

        def widest(s, rows):
            top = s[:, :HD]
            for t in range(1, s.shape[1] // HD):
                top = jnp.maximum(top, s[:, t * HD : (t + 1) * HD])
            mx[rows, :] = jnp.maximum(mx[rows, :], top)

        def score_prior(jp, cr):
            keys = kvb[pl.ds(pl.multiple_of(jp * PCH, PCH), PCH), pl.ds(0, HD)]
            for h in range(REP):
                rows = pl.ds(h * BLK, BLK)
                s = dot_t(q4[i, rows, :], keys) * C2
                s = jnp.where(iota(s.shape, 1) < c * BSP - jp * PCH, s, -jnp.inf)
                sbuf[0, rows, pl.ds(pl.multiple_of(jp * PCH, PCH), PCH)] = s
                widest(s, rows)
            return cr

        lax.fori_loop(0, n_chunk, score_prior, 0)

        def score(j, masked):
            keys = kv[pl.ds(pl.multiple_of(j * STEP, STEP), STEP), pl.ds(0, HD)]
            for h in range(REP):
                rows = pl.ds(h * BLK, BLK)
                s = dot_t(q4[i, rows, :], keys) * C2
                if masked:
                    s = jnp.where(iota(s.shape, 1) - iota(s.shape, 0) <= z * BLK, s, -jnp.inf)
                sbuf[1 + j, rows, :] = s
                widest(s, rows)

        def score_full(j, cr):
            score(j, False)
            return cr

        lax.fori_loop(0, i, score_full, 0)
        score(i, True)

        peak = jnp.max(mx[...], axis=1, keepdims=True)
        mx[...] = jnp.broadcast_to(peak, (ROWS, HD))
        acc[...] = jnp.zeros((ROWS, 2 * HD), jnp.float32)

        def spread(s, rows):
            m = mx[rows, :]
            return jnp.concatenate(
                [jnp.exp2(s[:, t * HD : (t + 1) * HD] - m) for t in range(s.shape[1] // HD)], axis=1
            ).astype(jnp.bfloat16)

        def mix_prior(jp, cr):
            at = pl.ds(pl.multiple_of(jp * PCH, PCH), PCH)
            vals = kvb[at, pl.ds(HD, 2 * HD)]
            for h in range(REP):
                rows = pl.ds(h * BLK, BLK)
                acc[rows, :] += dot_n(spread(sbuf[0, rows, at], rows), vals)
            return cr

        lax.fori_loop(0, n_chunk, mix_prior, 0)

        def mix(j, cr):
            vals = kv[pl.ds(pl.multiple_of(j * STEP, STEP), STEP), pl.ds(HD, 2 * HD)]
            for h in range(REP):
                rows = pl.ds(h * BLK, BLK)
                acc[rows, :] += dot_n(spread(sbuf[1 + j, rows, :], rows), vals)
            return cr

        lax.fori_loop(0, i + 1, mix, 0)
        eye = iota((HD, HD), 0) == iota((HD, HD), 1)
        for h in range(REP):
            rows = pl.ds(h * BLK, BLK)
            total = acc[rows, pl.ds(HD, HD)]
            outg[pl.ds(i * BLK, BLK), pl.ds(h * HD, HD)] = (acc[rows, pl.ds(0, HD)] / total).astype(jnp.bfloat16)
            lse = mx[rows, :] + jnp.log2(total)
            for t in range(BLK // HD):
                part = jnp.where(eye, lse[t * HD : (t + 1) * HD], 0.0)
                lse_row[i, :, pl.ds(h * BLK + t * HD, HD)] = jnp.sum(part, axis=0, keepdims=True)
        for cc in range(NC):
            grp = i * NC + cc

            @pl.when(grp != g)
            def _():
                if COMM:
                    o_send(grp).start()

            @pl.when(grp == g)
            def _():
                cols = pl.ds(pl.multiple_of(g * REP * HD, REP * HD), REP * HD)
                pltpu.make_async_copy(piece_q(outg, g), out_hbm.at[:, cols], o_r.at[g]).start()

        return carry

    lax.fori_loop(0, NX, block, 0)

    def deltas(i, carry):
        for cc in range(NC):
            grp = i * NC + cc
            if COMM:
                wait_group(functools.partial(piece_q, dog), do_r, grp)
            else:
                pl.when(grp == g)(lambda: wait_group(functools.partial(piece_q, dog), do_r, g))
        eye = iota((HD, HD), 0) == iota((HD, HD), 1)
        for h in range(REP):
            cols = pl.ds(h * HD, HD)
            grad = dog[pl.ds(i * BLK, BLK), cols]
            do4[i, pl.ds(h * BLK, BLK), :] = grad
            prod = grad.astype(jnp.float32) * outg[pl.ds(i * BLK, BLK), cols].astype(jnp.float32)
            total = jnp.broadcast_to(jnp.sum(prod, axis=1, keepdims=True), prod.shape)
            for t in range(BLK // HD):
                part = jnp.where(eye, total[t * HD : (t + 1) * HD], 0.0)
                del_row[i, :, pl.ds(h * BLK + t * HD, HD)] = jnp.sum(part, axis=0, keepdims=True)

        return carry

    lax.fori_loop(0, NX, deltas, 0)

    def back(cp, carry):
        at = pl.ds(pl.multiple_of(cp * 256, 256), 256)
        rel = own + cp * 256 - c * BSP
        place = (rel % 32 // 8) * STEP + (rel // 32) * BLK + (rel % 8) * 32 + 31
        place = jnp.where(rel < 0, -1, jnp.where(rel >= BSP, LOC, place))
        keys, vals = kvb[at, pl.ds(0, HD)], kvb[at, pl.ds(HD, HD)]
        dk_acc[...] = jnp.zeros((256, HD), jnp.float32)
        dv_acc[...] = jnp.zeros((256, HD), jnp.float32)

        def one(i, cr):
            for h in range(REP):
                rows = pl.ds(h * BLK, BLK)
                qs, gs = q4[i, rows, :], do4[i, rows, :]
                here = iota((1, BLK), 1) + i * STEP + z * BLK
                p = jnp.where(place <= here, jnp.exp2(dot_t(keys, qs) * C2 - lse_row[i, :, rows]), 0.0)
                dsb[:, rows] = (p * (dot_t(vals, gs) - del_row[i, :, rows])).astype(jnp.bfloat16)
                pb[:, rows] = p.astype(jnp.bfloat16)
            dv_acc[...] += dot_n(pb[...], do4[i])
            dk_acc[...] += dot_n(dsb[...], q4[i])
            return cr

        lax.fori_loop(0, NX, one, 0)
        for a in range(2):
            for zz in range(NZ):
                s = (cp * 2 + a) * NZ + zz
                rows = pl.ds(a * BSP + zz * BEA, BEA)
                gacc[s, pl.ds(0, BEA), :] = (dk_acc[rows, :] * SCALE).astype(jnp.bfloat16)
                gacc[s, pl.ds(BEA, BEA), :] = dv_acc[rows, :].astype(jnp.bfloat16)

                @pl.when(s == me)
                def _():
                    gown[pl.ds(0, BEA), :] = dk_acc[rows, :] * SCALE
                    gown[pl.ds(BEA, BEA), :] = dv_acc[rows, :]

        if COMM:
            plane(cp * 2 * NZ, jnp.minimum(cp * 2 + 2, c + 1) * NZ, lambda s: g_send(s).start())
        return carry

    if BWD:
        lax.fori_loop(0, n_back, back, 0)

        row = iota((HD, 1), 0)
        dest, head, num = row // 16, (row // 4) % 4, row % 4
        spot = head * BLK + (dest % NC) * TOK + num * 32 + 31
        here = (dest // NC) * STEP + z * BLK + (dest % NC) * TOK + num * 32 + 31
        qb = jnp.zeros((HD, HD), jnp.float32)
        gb = jnp.zeros((HD, HD), jnp.float32)
        lse_b = jnp.zeros((HD, 1), jnp.float32)
        del_b = jnp.zeros((HD, 1), jnp.float32)
        for i in range(NX):
            pick = (iota((HD, ROWS), 1) == spot) & (dest // NC == i)
            hot = pick.astype(jnp.bfloat16)
            qb = qb + dot_n(hot, q4[i])
            gb = gb + dot_n(hot, do4[i])
            lse_b = lse_b + jnp.sum(jnp.where(pick, lse_row[i], 0.0), axis=1, keepdims=True)
            del_b = del_b + jnp.sum(jnp.where(pick, del_row[i], 0.0), axis=1, keepdims=True)
        qb = qb.astype(jnp.bfloat16)
        gb = gb.astype(jnp.bfloat16)

        def dq_part(keys, vals, seen):
            s = dot_t(qb, keys)
            p = jnp.where(seen(iota(s.shape, 1)), jnp.exp2(s * C2 - lse_b), 0.0)
            ds = (p * (dot_t(gb, vals) - del_b)).astype(jnp.bfloat16)
            return dot_n(ds, keys)

        def dq_prior(jp, total):
            at = pl.ds(pl.multiple_of(jp * 256, 256), 256)
            seen = lambda col: col < c * BSP - jp * 256
            return total + dq_part(kvb[at, pl.ds(0, HD)], kvb[at, pl.ds(HD, HD)], seen)

        dq = lax.fori_loop(0, n_prior, dq_prior, jnp.zeros((HD, HD), jnp.float32))

        def dq_local(j, total):
            at = pl.ds(pl.multiple_of(j * STEP, STEP), STEP)
            seen = lambda col: col + j * STEP <= here
            return total + dq_part(kv[at, pl.ds(0, HD)], kv[at, pl.ds(HD, HD)], seen)

        dq = lax.fori_loop(0, NX, dq_local, dq)
        dq_st[...] = dq * SCALE
    mine_rows = pl.ds(pl.multiple_of(g * 16, 16), 16)
    gq_in[mine_rows, :] = dq_st[mine_rows, :]
    if COMM:
        others(lambda grp: d_send(grp).start())

    if COMM:

        def add(s):
            arrived(slots.at[s], g_r.at[s])
            gown[...] += slots[s].astype(jnp.float32)

        plane(c * NZ, PLANE, add)
    for d in range(NG):
        tiles[d, pl.ds(0, 4), :] = gown[pl.ds(d * 4, 4), :]
        tiles[d, pl.ds(4, 4), :] = gown[pl.ds(BEA + d * 4, 4), :]
    gkv_in[g] = tiles[g]
    if COMM:
        others(lambda grp: t_send(grp).start())
        others(lambda grp: arrived(gq_in.at[pl.ds(pl.multiple_of(grp * 16, 16), 16), :], d_r.at[grp]))
        others(lambda grp: arrived(gkv_in.at[grp], t_r.at[grp]))
    for grp in range(NG):
        gk_ref[:, pl.ds(grp * HD, HD)] = gkv_in[grp, pl.ds(0, 4), :]
        gv_ref[:, pl.ds(grp * HD, HD)] = gkv_in[grp, pl.ds(4, 4), :]
        for h in range(REP):
            gq_ref[:, pl.ds((grp * REP + h) * HD, HD)] = gq_in[pl.ds(grp * 16 + h * 4, 4), :]

    def out_cols(grp):
        return out_hbm.at[:, pl.ds(pl.multiple_of(grp * REP * HD, REP * HD), REP * HD)]

    if FWD:
        arrived(out_cols(g), o_r.at[g])
    if COMM:
        others(lambda grp: arrived(out_cols(grp), o_r.at[grp]))
        for which in range(4):
            others(lambda grp, which=which: remote(*x_copies(grp)[which], in_group(grp)).wait_send())
        for xx in range(NX):
            for way in range(2):
                z_send(xx, way).wait_send()
                z_relay(xx, way).wait_send()
        plane(c * NZ, PLANE, lambda s: b_send(s).wait_send())
        others(lambda grp: o_send(grp).wait_send())
        plane(0, (c + 1) * NZ, lambda s: g_send(s).wait_send())
        others(lambda grp: d_send(grp).wait_send())
        others(lambda grp: t_send(grp).wait_send())


def on_device(query, key, value, d_out):
    f32, b16 = jnp.float32, jnp.bfloat16
    vm = pltpu.VMEM
    dma = pltpu.SemaphoreType.DMA
    scratch = [
        vm((LOC, 3 * HD), b16), vm((ALLB, 3 * HD), b16), vm((BEA, 2 * HD), b16),
        vm((NX * BLK, REP * HD), b16), vm((NX * BLK, REP * HD), b16), vm((NX * BLK, REP * HD), b16),
        vm((NX, ROWS, HD), b16), vm((NX, ROWS, HD), b16),
        vm((1 + NX, ROWS, STEP), f32), vm((ROWS, HD), f32), vm((ROWS, 2 * HD), f32),
        vm((NX, 1, ROWS), f32), vm((NX, 1, ROWS), f32),
        vm((256, HD), f32), vm((256, HD), f32), vm((256, ROWS), b16), vm((256, ROWS), b16), vm((2 * BEA, HD), f32), vm((PLANE, 2 * BEA, HD), b16), vm((PLANE, 2 * BEA, HD), b16),
        vm((NG, 8, HD), f32), vm((NG, 8, HD), f32), vm((HD, HD), f32), vm((HD, HD), f32),
        dma((NG,)), dma((NG,)), dma((NG,)), dma((NG,)), dma((NG,)), dma((NG,)), dma((NG,)), dma((NG,)),
        dma((NX, 2)), dma((NX, 4)), dma((NX, 2)), dma((PLANE,)), dma((PLANE,)),
        dma((NG,)), dma((NG,)), dma((PLANE,)), dma((PLANE,)), dma((NG,)), dma((NG,)), dma((NG,)), dma((NG,)),
    ]
    anyspace = pl.BlockSpec(memory_space=pl.ANY)
    inner = pl.BlockSpec(memory_space=pltpu.VMEM)
    return pl.pallas_call(
        fused,
        out_shape=(
            jax.ShapeDtypeStruct((TOK, NG * REP * HD), b16),
            jax.ShapeDtypeStruct((4, NG * REP * HD), f32),
            jax.ShapeDtypeStruct((4, NG * HD), f32),
            jax.ShapeDtypeStruct((4, NG * HD), f32),
        ),
        in_specs=[anyspace] * 4,
        out_specs=(anyspace, inner, inner, inner),
        scratch_shapes=scratch,
        compiler_params=pltpu.CompilerParams(
            collective_id=0 if COMM else None, has_side_effects=True, vmem_limit_bytes=60 * 1024 * 1024
        ),
    )(query, key, value, d_out)


def solution(mesh):
    spec = P(("span", "ulysses"), None)
    return jax.shard_map(
        on_device, mesh=mesh, in_specs=(spec,) * 4, out_specs=(spec,) * 4, check_vma=False
    )
```
